256 devices in a mesh: view: 64 (over z, y, core), feat: 4 (over x).
Axes of the slice: x: 4, y: 4, z: 8, core: 2. Of those that a mesh axis runs over, the one named last changes fastest.
Arguments:
- points: bfloat16 [4096, 768, 128], P('view', 'feat'), may hold values from -6 to 6
- head_weight: bfloat16 [768, 768], P('feat'), may hold values from -0.21875 to 0.21875
- teacher: bfloat16 [768, 128, 1369], P('feat', 'view'), may hold values from -6 to 6
- splat_weight: bfloat16 [128, 64, 74, 128], P('view'), may hold values from 0 to 0.19921875
- block_owner: int32 [128, 16, 4], P('view'), may hold values from 0 to 63, all different within a row; in each aligned block of 32 rows (0 to 31, 32 to 63, ..., all dimensions but the last counted through in order) at most 3 rows name the same one
- block_local: int32 [128, 64], P('view'), may hold values from 0 to 63
- block_row: int32 [128, 64], P('view'), may hold values from 0 to 35, as said below
Outputs:
- grad_points: bfloat16 [4096, 768, 128], P('view', 'feat')
- head_grad: float32 [768, 768], P('feat')
The draws below stay inside these ranges and needn't reach their ends.
Inputs may be any that keep to these rules, and one draw needn't show every extreme that they name: `block_owner`: over the 128 list entries of the views of one index of view, no owner appears more than 3 times, and some owner appears exactly 3 times. `block_row`: each view's list holds every value from 0 to 35 at least once.
All inputs are finite; a program needn't handle non-finite values.
Results may differ from the reference program's by a relative error of at most 0.0064.
Values may be sent and summed in bfloat16 or wider, within the bound.
A program may use at most 128 MiB of HBM per device.

```python
import math
import jax
import jax.numpy as jnp
import numpy as np
from jax import lax

D = 768
DT = 768
GRID = 37
BAND = 2
BLOCK = 128
VIEW_DEV = 2
NVIS = 64
BLK_DEV = 64
VIEWS = 128
NBLK = 4096
PIX = 1369
CAP = 3
N_VIEW = 64


def draw_block_row(key, part):
    row_range = GRID - BAND + 1
    view_keys = jax.random.split(key, VIEWS)
    leading = jax.vmap(lambda view_key: jax.random.permutation(view_key, row_range))(view_keys).astype(jnp.int32)
    others = jax.random.randint(jax.random.fold_in(key, 7), (VIEWS, NVIS - row_range), 0, row_range, dtype=jnp.int32)
    return jnp.concatenate([leading, others], axis=1)


def plant(entries, stream_key, smallest, largest):
    dims = entries.shape
    place = [jax.random.randint(jax.random.fold_in(stream_key, axis), (), 0, dims[axis]) for axis in range(len(dims))]
    entries = entries.at[tuple(place)].set(smallest)
    longest = dims.index(max(dims))
    place[longest] = (place[longest] + 1) % dims[longest]
    return entries.at[tuple(place)].set(largest)


def steps_of(rng, shape, cuts, low, top_value):
    def one(axis_at, shards_of):
        heights = jax.random.uniform(jax.random.fold_in(jax.random.fold_in(rng, 6), axis_at), (shards_of,), jnp.float32, low / len(cuts), top_value / len(cuts))
        return jnp.repeat(jnp.exp(heights), shape[axis_at] // shards_of).reshape((-1,) + (1,) * (len(shape) - axis_at - 1))

    level = one(*cuts[0])
    for cut in cuts[1:]:
        level = level * one(*cut)
    return level


def shared_out(own_key, own, number, rows, amount, top, most, slope):
    ranking = jax.random.permutation(own_key, amount)
    crowded, ordinary = portions_of(amount, rows * top, most, slope, True), portions_of(amount, rows * top, most, slope, False)
    places = jnp.arange(amount)

    def named(sizes, offset_by):
        used = int((sizes > 0).sum())
        fixed = max(1, used // 4)
        moved = fixed + (places - fixed + offset_by * (used - fixed)) % max(1, amount - fixed)
        return jnp.zeros((amount,), jnp.int32).at[ranking[jnp.where(places < fixed, places, moved)]].set(jnp.asarray(sizes, jnp.int32))

    sizes = jnp.where(number % 4 == 0, named(crowded, number // 4), named(ordinary, number - number // 4 - 1))
    mixed = jax.random.permutation(jax.random.fold_in(own, 3), amount)
    source_of, receiver = mixed[0:amount // 2 * 2:2], mixed[1:amount // 2 * 2:2]
    margin = jnp.minimum(sizes[source_of] - 1, most - sizes[receiver]) // 2
    margin = jnp.where((source_of == ranking[0]) | (receiver == ranking[0]) | (sizes[receiver] == 0), 0, jnp.maximum(margin, 0))
    moved = jax.random.randint(jax.random.fold_in(own, 4), (amount // 2,), 0, 1 << 20) % (margin + 1)
    sizes = sizes.at[source_of].add(-moved).at[receiver].add(moved)
    items = jnp.searchsorted(jnp.cumsum(sizes), jnp.arange(rows * top), side="right").astype(jnp.int32)
    table = items.reshape(top, rows).T
    table = table[jax.random.permutation(jax.random.fold_in(own, 1), rows)]
    offset_by = jax.random.randint(jax.random.fold_in(own, 2), (rows, 1), 0, top)
    return jnp.take_along_axis(table, (jnp.arange(top)[None, :] + offset_by) % top, axis=1)


def portions_of(number_of, total, limit, skew, full):
    weights = [(1 << 20) // math.isqrt(grade ** skew) + 1 for grade in range(1, number_of + 1)]
    largest = limit if full else min(limit, max(-(-total // number_of), total * weights[0] // sum(weights)))
    least = 1 if total - largest >= number_of - 1 else 0
    given, spare = [largest] + [least] * (number_of - 1), total - largest - least * (number_of - 1)
    while spare > 0:
        free = [i for i in range(1, number_of) if given[i] < largest] or [i for i in range(1, number_of) if given[i] < limit]
        pool, remaining = sum([weights[i] for i in free]), spare
        for i in free:
            addition = min(limit - given[i], max(1, remaining * weights[i] // pool), spare)
            given[i] = given[i] + addition
            spare = spare - addition
    return np.array(given)


def scatter_about(key, extent, width, limit, cuts=(), held_as=jnp.bfloat16):
    level = steps_of(key, extent, cuts, -0.22, 0.18) if cuts else 1.0
    result = jax.random.normal(key, extent, jnp.float32) * width * level
    return jnp.minimum(jnp.maximum(result, -limit), limit).astype(held_as)


def setup_inputs(seed: int = 0) -> dict:
    key_of = jax.random.split(jax.random.key(seed), 8)
    points = scatter_about(key_of[0], (NBLK, D, BLOCK), 1.0, 6.0, ((0, 64), (1, 4)))
    head_weight = scatter_about(key_of[1], (D, DT), D ** -0.5, 0.21875, ((0, 4),))
    teacher = scatter_about(key_of[2], (DT, VIEWS, PIX), 1.0, 6.0, ((0, 4), (1, 64)))
    splat_weight = jnp.clip(0.19921875 * jax.random.uniform(key_of[3], (VIEWS, NVIS, BAND * GRID, BLOCK), jnp.float32) ** steps_of(key_of[3], (VIEWS, NVIS, BAND * GRID, BLOCK), ((0, 64),), -0.2, 0.2), 0.0, 0.19921875).astype(jnp.bfloat16)
    block_owner_keys = jax.random.split(jax.random.fold_in(key_of[4], 1), VIEWS * (NVIS // 4) // (VIEW_DEV * NVIS // 4))
    block_owner_turns = jax.random.permutation(jax.random.fold_in(key_of[4], 3), VIEWS * (NVIS // 4) // (VIEW_DEV * NVIS // 4))
    block_owner = jax.vmap(lambda own, number: shared_out(jax.random.fold_in(key_of[4], 2), own, number, VIEW_DEV * NVIS // 4, N_VIEW, 4, CAP, 2))(block_owner_keys, block_owner_turns).reshape((VIEWS, NVIS // 4, 4))
    block_local = plant(jax.random.randint(key_of[5], (VIEWS, NVIS), 0, BLK_DEV), jax.random.fold_in(key_of[5], 1), 0, BLK_DEV - 1).astype(jnp.int32)
    block_row = draw_block_row(jax.random.fold_in(key_of[7], 71), 0)
    return {"points": points, "head_weight": head_weight, "teacher": teacher, "splat_weight": splat_weight, "block_owner": block_owner, "block_local": block_local, "block_row": block_row}


def reference(points, head_weight, teacher, splat_weight, block_owner, block_local, block_row):
    blocks = points
    owners = block_owner.reshape(VIEWS, NVIS)
    global_ids = (owners * BLK_DEV + block_local).astype(jnp.int32)
    teacher_views = jnp.moveaxis(teacher, 1, 0)
    columns = jnp.arange(GRID, dtype=jnp.int32)

    def one_view(state_pair, inputs):
        grad_acc, head_acc = state_pair
        weights, view_ids, top_rows, target_feat = inputs
        fetched = blocks[view_ids]
        contrib = jnp.einsum('jcp,jdp->jcd', weights.astype(jnp.float32), fetched.astype(jnp.float32)).astype(jnp.bfloat16)
        rendered = jnp.zeros((GRID, GRID, D), jnp.float32)
        row_masks = []
        for offset in range(BAND):
            row_mask = (top_rows[:, None] + offset == columns[None, :]).astype(jnp.float32)
            row_masks.append(row_mask)
            band_part = contrib[:, offset * GRID:(offset + 1) * GRID, :].astype(jnp.float32)
            rendered = rendered + jnp.einsum('jr,jcd->rcd', row_mask, band_part)
        rendered = rendered.astype(jnp.bfloat16).reshape(PIX, D)
        projected = jnp.dot(rendered, head_weight, preferred_element_type=jnp.float32)
        scale_rows = jnp.sqrt(lax.optimization_barrier(jnp.mean(projected * projected, axis=1, keepdims=True)) + 1e-06)
        normed = projected / scale_rows
        residual = normed - target_feat.T.astype(jnp.float32)
        row_dot = lax.optimization_barrier(jnp.mean(residual * normed, axis=1, keepdims=True))
        grad_proj = ((residual - normed * row_dot) / scale_rows).astype(jnp.bfloat16)
        grad_image = jnp.dot(grad_proj, head_weight.T, preferred_element_type=jnp.float32).astype(jnp.bfloat16)
        grad_image = grad_image.reshape(GRID, GRID, D).astype(jnp.float32)
        grad_head = jnp.dot(rendered.T, grad_proj, preferred_element_type=jnp.float32)
        pieces = [jnp.einsum('jr,rcd->jcd', row_mask, grad_image) for row_mask in row_masks]
        grad_contrib = jnp.concatenate(pieces, axis=1).astype(jnp.bfloat16)
        grad_block = jnp.einsum('jcp,jcd->jdp', weights.astype(jnp.float32), grad_contrib.astype(jnp.float32)).astype(jnp.bfloat16)
        grad_acc = grad_acc.at[view_ids].add(grad_block.astype(jnp.float32))
        return ((grad_acc, head_acc + grad_head), None)
    start_state = (jnp.zeros((NBLK, D, BLOCK), jnp.float32), jnp.zeros((D, DT), jnp.float32))
    final_state, _ = lax.scan(one_view, start_state, (splat_weight, global_ids, block_row, teacher_views))
    grad_acc, head_acc = final_state
    grad_points = grad_acc.astype(jnp.bfloat16)
    head_grad = head_acc / (VIEWS * GRID)
    return (grad_points, head_grad)
```

```python
import functools

import jax
import jax.numpy as jnp
from jax import lax
from jax.experimental import pallas as pl
from jax.experimental.pallas import tpu as pltpu
from jax.sharding import PartitionSpec as P

GRID = 37
BAND = 2
BLOCK = 128
CAP = 3
ROWS = BAND * GRID
PIECE = 24
SLOT = 112
LINE = 40
STEP = 8
SMEM = functools.partial(pl.BlockSpec, memory_space=pltpu.SMEM)
NT = (((1,), (1,)), ((), ()))
TN = (((0,), (0,)), ((), ()))
VMEM_LIMIT = 60 * 1024 * 1024


def params(**kw):
    return pltpu.CompilerParams(vmem_limit_bytes=VMEM_LIMIT, **kw)


def slot_plan(owners, peer_count, capacity):
    total_requests = owners.shape[0]
    positions = jnp.arange(total_requests, dtype=jnp.int32)
    earlier = (owners[:, None] == owners[None, :]) & (positions[None, :] < positions[:, None])
    slot_rank = jnp.sum(earlier.astype(jnp.int32), axis=1)
    target = owners * capacity + slot_rank
    slot_ids = jnp.arange(peer_count * capacity, dtype=jnp.int32)
    matches = target[None, :] == slot_ids[:, None]
    source = jnp.sum(jnp.where(matches, positions[None, :], 0), axis=1)
    filled = jnp.any(matches, axis=1)
    return source, filled.astype(jnp.int32)


def pack_weights_kernel(source, filled, local, last, weights, out):
    step = pl.program_id(0)
    row = lax.broadcasted_iota(jnp.int32, (PIECE, BLOCK), 0)

    def one(i, carry):
        for s in range(CAP):
            t = (step * STEP + i) * CAP + s
            src = source[t]
            piece = weights[src].astype(jnp.float32)
            piece = jnp.where(filled[t] > 0, piece, 0.0)
            tag = local[src].astype(jnp.float32)
            piece = jnp.where((row == PIECE - 1) & (last[0] > 0), tag, piece)
            out[i, pl.ds(s * PIECE, PIECE), :] = piece.astype(jnp.bfloat16)
        return carry

    lax.fori_loop(0, STEP, one, 0)


def pack_weights(source, filled, local, last, weights, peers):
    return pl.pallas_call(
        pack_weights_kernel,
        out_shape=jax.ShapeDtypeStruct((peers, CAP * PIECE, BLOCK), jnp.bfloat16),
        grid=(peers // STEP,),
        in_specs=[SMEM(), SMEM(), SMEM(), SMEM(), pl.BlockSpec(weights.shape, lambda i: (0, 0, 0))],
        out_specs=pl.BlockSpec((STEP, CAP * PIECE, BLOCK), lambda i: (i, 0, 0)),
        compiler_params=params(),
        name="pack_weights",
    )(source, filled, local, last, weights)


def slot_weights(pieces, i, s):
    base = s * PIECE
    parts = [pieces[f, i, pl.ds(base, PIECE), :] for f in range(3)]
    parts.append(pieces[3, i, pl.ds(base, 8), :])
    return jnp.concatenate([p.astype(jnp.float32) for p in parts], axis=0).astype(jnp.bfloat16)


def splat_kernel(ids, points, pieces, out, buf):
    step = pl.program_id(0)
    lane = lax.broadcasted_iota(jnp.int32, (GRID, BLOCK), 1)

    def one(i, carry):
        for s in range(CAP):
            block = points[ids[(step * STEP + i) * CAP + s]]
            wide = jnp.concatenate([block, block[128:192]], axis=0)
            product = lax.dot_general(slot_weights(pieces, i, s), wide, NT, preferred_element_type=jnp.float32)
            rest = product[:, 128:256]
            buf[s, 0:80, :] = product[:, 0:128]
            buf[s, ROWS : ROWS + GRID, :] = jnp.where(lane < 64, rest[0:GRID], rest[GRID:ROWS])
            buf[s, SLOT - 1 : SLOT, :] = jnp.zeros((1, BLOCK), jnp.float32)
            out[i, pl.ds(s * SLOT, SLOT), :] = buf[s].astype(jnp.bfloat16)
        return carry

    lax.fori_loop(0, STEP, one, 0)


def splat(ids, points, pieces):
    peers = pieces.shape[1]
    return pl.pallas_call(
        splat_kernel,
        out_shape=jax.ShapeDtypeStruct((peers, CAP * SLOT, BLOCK), jnp.bfloat16),
        grid=(peers // STEP,),
        in_specs=[
            SMEM(),
            pl.BlockSpec(points.shape, lambda i: (0, 0, 0)),
            pl.BlockSpec((4, STEP, CAP * PIECE, BLOCK), lambda i: (0, i, 0, 0)),
        ],
        out_specs=pl.BlockSpec((STEP, CAP * SLOT, BLOCK), lambda i: (i, 0, 0)),
        scratch_shapes=[pltpu.VMEM((CAP, SLOT, BLOCK), jnp.float32)],
        compiler_params=params(),
        name="splat",
    )(ids, points, pieces)


def render_kernel(lines, source, line_of, arrived, out, acc):
    step = pl.program_id(0)

    @pl.when(step == 0)
    def _():
        acc[...] = jnp.zeros_like(acc)

    def one(i, carry):
        for s in range(CAP):
            at = line_of[source[(step * STEP + i) * CAP + s]] + 1
            acc[at] += arrived[i, pl.ds(s * SLOT, SLOT), :].astype(jnp.float32)
        return carry

    lax.fori_loop(0, STEP, one, 0)

    @pl.when(step == pl.num_programs(0) - 1)
    def _():
        def finish(k, carry):
            upper, own = acc[k], acc[k + 1]
            main = own[0:GRID] + upper[GRID:ROWS]
            pair = own[ROWS : ROWS + GRID] + pltpu.roll(upper, 64, 1)[ROWS : ROWS + GRID]
            out[k, 0:GRID, 0:128] = main.astype(jnp.bfloat16)
            out[k, 0:GRID, 128:192] = pair[:, 0:64].astype(jnp.bfloat16)
            return carry

        out[...] = jnp.zeros_like(out)
        lax.fori_loop(0, lines, finish, 0)


def render(source, line_of, arrived, lines, padded):
    peers = arrived.shape[0]
    return pl.pallas_call(
        functools.partial(render_kernel, lines),
        out_shape=jax.ShapeDtypeStruct((padded, LINE, 192), jnp.bfloat16),
        grid=(peers // STEP,),
        in_specs=[SMEM(), SMEM(), pl.BlockSpec((STEP, CAP * SLOT, BLOCK), lambda i: (i, 0, 0))],
        out_specs=pl.BlockSpec((padded, LINE, 192), lambda i: (0, 0, 0)),
        scratch_shapes=[pltpu.VMEM((lines + 1, SLOT, BLOCK), jnp.float32)],
        compiler_params=params(),
        name="render",
    )(source, line_of, arrived)


def compare_kernel(rendered, head, target, grad_image, grad_proj):
    width = target.shape[1]
    projected = jnp.zeros(target.shape, jnp.float32)
    for f in range(4):
        projected += jnp.dot(rendered[f], head[f], preferred_element_type=jnp.float32)
    scale = jnp.sqrt(jnp.sum(projected * projected, axis=1, keepdims=True) / width + 1e-06)
    inverse = 1.0 / scale
    normed = projected * inverse
    residual = normed - target[...].astype(jnp.float32)
    row_dot = jnp.sum(residual * normed, axis=1, keepdims=True) / width
    grad = ((residual - normed * row_dot) * inverse).astype(jnp.bfloat16)
    grad_proj[...] = grad
    for f in range(4):
        grad_image[f] = lax.dot_general(grad, head[f], NT, preferred_element_type=jnp.float32).astype(jnp.bfloat16)


def compare(rendered, head, target):
    rows, width = target.shape
    part = rows // 5
    return pl.pallas_call(
        compare_kernel,
        out_shape=(
            jax.ShapeDtypeStruct(rendered.shape, jnp.bfloat16),
            jax.ShapeDtypeStruct(target.shape, jnp.bfloat16),
        ),
        grid=(5,),
        in_specs=[
            pl.BlockSpec((4, part, 192), lambda i: (0, i, 0)),
            pl.BlockSpec(head.shape, lambda i: (0, 0, 0)),
            pl.BlockSpec((part, width), lambda i: (i, 0)),
        ],
        out_specs=(
            pl.BlockSpec((4, part, 192), lambda i: (0, i, 0)),
            pl.BlockSpec((part, width), lambda i: (i, 0)),
        ),
        compiler_params=params(),
        name="compare",
    )(rendered, head, target)


def pack_grads_kernel(lines, source, line_of, image, out, slots, buf):
    step = pl.program_id(0)

    @pl.when(step == 0)
    def _():
        def build(k, carry):
            own, lower = image[k].astype(jnp.float32), image[k + 1].astype(jnp.float32)
            buf[0:GRID, :] = own[0:GRID, 0:128]
            buf[GRID:ROWS, :] = lower[0:GRID, 0:128]
            pair = jnp.concatenate([own[0:GRID, 128:192], lower[0:GRID, 128:192]], axis=1)
            buf[ROWS : ROWS + GRID, :] = pair
            slots[k] = buf[...].astype(jnp.bfloat16)
            return carry

        buf[...] = jnp.zeros_like(buf)
        lax.fori_loop(0, lines, build, 0)

    def one(i, carry):
        for s in range(CAP):
            out[i, pl.ds(s * SLOT, SLOT), :] = slots[line_of[source[(step * STEP + i) * CAP + s]]]
        return carry

    lax.fori_loop(0, STEP, one, 0)


def pack_grads(source, line_of, image, peers, lines):
    return pl.pallas_call(
        functools.partial(pack_grads_kernel, lines),
        out_shape=jax.ShapeDtypeStruct((peers, CAP * SLOT, BLOCK), jnp.bfloat16),
        grid=(peers // STEP,),
        in_specs=[SMEM(), SMEM(), pl.BlockSpec(image.shape, lambda i: (0, 0, 0))],
        out_specs=pl.BlockSpec((STEP, CAP * SLOT, BLOCK), lambda i: (i, 0, 0)),
        scratch_shapes=[
            pltpu.VMEM((lines, SLOT, BLOCK), jnp.bfloat16),
            pltpu.VMEM((SLOT, BLOCK), jnp.float32),
        ],
        compiler_params=params(),
        name="pack_grads",
    )(source, line_of, image)


def unsplat_kernel(ids, pieces, arrived, out, acc):
    step = pl.program_id(0)
    lane = lax.broadcasted_iota(jnp.int32, (GRID, BLOCK), 1)

    @pl.when(step == 0)
    def _():
        acc[...] = jnp.zeros_like(acc)

    def one(i, carry):
        for s in range(CAP):
            at = ids[(step * STEP + i) * CAP + s]
            weights = slot_weights(pieces, i, s)
            slot = arrived[i, pl.ds(s * SLOT, SLOT), :].astype(jnp.float32)
            pair = slot[ROWS : ROWS + GRID]
            rest = jnp.concatenate(
                [jnp.where(lane < 64, pair, 0.0), jnp.where(lane < 64, 0.0, pair), jnp.zeros((6, BLOCK), jnp.float32)], axis=0
            )
            both = jnp.concatenate([slot[0:80], rest], axis=1).astype(jnp.bfloat16)
            product = lax.dot_general(both, weights, TN, preferred_element_type=jnp.float32)
            acc[at, 0:128, :] += product[0:128].astype(jnp.bfloat16).astype(jnp.float32)
            acc[at, 128:192, :] += (product[128:192] + product[192:256]).astype(jnp.bfloat16).astype(jnp.float32)
        return carry

    lax.fori_loop(0, STEP, one, 0)

    @pl.when(step == pl.num_programs(0) - 1)
    def _():
        out[...] = acc[...].astype(jnp.bfloat16)


def unsplat(ids, pieces, arrived, shape):
    peers = arrived.shape[0]
    return pl.pallas_call(
        unsplat_kernel,
        out_shape=jax.ShapeDtypeStruct(shape, jnp.bfloat16),
        grid=(peers // STEP,),
        in_specs=[
            SMEM(),
            pl.BlockSpec((4, STEP, CAP * PIECE, BLOCK), lambda i: (0, i, 0, 0)),
            pl.BlockSpec((STEP, CAP * SLOT, BLOCK), lambda i: (i, 0, 0)),
        ],
        out_specs=pl.BlockSpec(shape, lambda i: (0, 0, 0)),
        scratch_shapes=[pltpu.VMEM(shape, jnp.float32)],
        compiler_params=params(),
        name="unsplat",
    )(ids, pieces, arrived)


def per_device(points, head_weight, teacher, splat_weight, block_owner, block_local, block_row):
    peers = lax.axis_size("view")
    feat = lax.axis_index("feat")
    local_width = points.shape[1]
    views, visible = splat_weight.shape[:2]
    requests = views * visible
    lines = views * GRID
    share = -(-lines // 4)
    padded = 4 * share
    rows = share * LINE

    source, filled = slot_plan(block_owner.reshape(requests), peers, CAP)
    local = block_local.reshape(requests)
    line_of = (block_row + jnp.arange(views, dtype=jnp.int32)[:, None] * GRID).reshape(requests)
    last = (feat == 3).astype(jnp.int32).reshape(1)

    mine = lax.dynamic_slice_in_dim(
        jnp.pad(splat_weight, ((0, 0), (0, 0), (0, 4 * PIECE - ROWS), (0, 0))), feat * PIECE, PIECE, axis=2
    ).reshape(requests, PIECE, BLOCK)
    packed = pack_weights(source, filled, local, last, mine, peers)
    swapped = lax.all_to_all(packed, "view", split_axis=0, concat_axis=0, tiled=True)
    pieces = lax.all_gather(swapped, "feat", axis=0)
    ids = pieces[3].reshape(peers, CAP, PIECE, BLOCK)[:, :, PIECE - 1, 0].astype(jnp.int32).reshape(peers * CAP)

    head = lax.all_gather(head_weight, "feat", axis=0)
    wanted = jnp.pad(
        teacher.reshape(local_width, lines, GRID), ((0, 0), (0, padded - lines), (0, LINE - GRID))
    ).reshape(local_width, 4, rows)
    target = lax.all_to_all(wanted.transpose(1, 0, 2), "feat", split_axis=0, concat_axis=0, tiled=True)
    target = target.reshape(4 * local_width, rows).T

    contrib = splat(ids, points, pieces)
    arrived = lax.all_to_all(contrib, "view", split_axis=0, concat_axis=0, tiled=True)
    image = render(source, line_of, arrived, lines, padded).reshape(4, rows, local_width)
    rendered = lax.all_to_all(image, "feat", split_axis=0, concat_axis=0, tiled=True)
    grad_image, grad_proj = compare(rendered, head, target)
    grad_rows = lax.all_to_all(grad_image, "feat", split_axis=0, concat_axis=0, tiled=True)
    grads = pack_grads(source, line_of, grad_rows.reshape(padded, LINE, local_width), peers, lines)
    landed = lax.all_to_all(grads, "view", split_axis=0, concat_axis=0, tiled=True)
    grad_points = unsplat(ids, pieces, landed, points.shape)

    head_part = jnp.einsum("frd,rt->fdt", rendered, grad_proj, preferred_element_type=jnp.float32)
    head_part = lax.psum_scatter(head_part, "feat", scatter_dimension=0, tiled=False)
    head_grad = lax.psum(head_part, "view") / (views * peers * GRID)
    return grad_points, head_grad


def solution(mesh):
    placed = (
        P("view", "feat", None),
        P("feat", None),
        P("feat", "view", None),
        P("view", None, None, None),
        P("view", None, None),
        P("view", None),
        P("view", None),
    )
    return jax.shard_map(
        per_device,
        mesh=mesh,
        in_specs=placed,
        out_specs=(P("view", "feat", None), P("feat", None)),
        check_vma=False,
    )
```

```python
import functools

import jax
import jax.numpy as jnp
from jax import lax
from jax.experimental import pallas as pl
from jax.experimental.pallas import tpu as pltpu
from jax.sharding import PartitionSpec as P

GRID = 37
BAND = 2
BLOCK = 128
CAP = 3
ROWS = BAND * GRID
PIECE = 24
SLOT = 112
LINE = 40
STEP = 8
STRIDE = 27
LAG = 12
MESH = pl.DeviceIdType.MESH
SMEM = functools.partial(pl.BlockSpec, memory_space=pltpu.SMEM)
NT = (((1,), (1,)), ((), ()))
TN = (((0,), (0,)), ((), ()))
VMEM_LIMIT = 60 * 1024 * 1024


def params(**kw):
    return pltpu.CompilerParams(vmem_limit_bytes=VMEM_LIMIT, **kw)


def slot_plan(owners, peer_count, capacity):
    total_requests = owners.shape[0]
    positions = jnp.arange(total_requests, dtype=jnp.int32)
    earlier = (owners[:, None] == owners[None, :]) & (positions[None, :] < positions[:, None])
    slot_rank = jnp.sum(earlier.astype(jnp.int32), axis=1)
    target = owners * capacity + slot_rank
    slot_ids = jnp.arange(peer_count * capacity, dtype=jnp.int32)
    matches = target[None, :] == slot_ids[:, None]
    source = jnp.sum(jnp.where(matches, positions[None, :], 0), axis=1)
    filled = jnp.any(matches, axis=1)
    return source, filled.astype(jnp.int32)


def peer_at(me, i, peers):
    return (me + i * STRIDE) % peers


def greet(me, feat, peers):
    barrier = pltpu.get_barrier_semaphore()

    def hello(i, carry):
        pl.semaphore_signal(barrier, inc=1, device_id=(peer_at(me, i, peers), feat), device_id_type=MESH)
        return carry

    lax.fori_loop(1, peers, hello, 0)
    for k in range(1, 4):
        pl.semaphore_signal(barrier, inc=1, device_id=(me, (feat + k) % 4), device_id_type=MESH)
    pl.semaphore_wait(barrier, peers + 2)


def remote(src, dst, send, recv, view, feat):
    return pltpu.make_async_remote_copy(
        src_ref=src, dst_ref=dst, send_sem=send, recv_sem=recv, device_id=(view, feat), device_id_type=MESH
    )


def wait_bytes(ref, sem):
    pltpu.make_async_copy(ref, ref, sem).wait()


def pack_weights_kernel(source, filled, local, weights, out, tags):
    step = pl.program_id(0)
    lane = lax.broadcasted_iota(jnp.int32, (1, BLOCK), 1)

    def one(i, carry):
        tag = jnp.zeros((1, BLOCK), jnp.int32)
        for s in range(CAP):
            t = (step * STEP + i) * CAP + s
            src = source[t]
            piece = jnp.where(filled[t] > 0, weights[src].astype(jnp.float32), 0.0)
            out[i, pl.ds(s * PIECE, PIECE), :] = piece.astype(jnp.bfloat16)
            tag = jnp.where(lane == s, local[src], tag)
        tags[i] = tag
        return carry

    lax.fori_loop(0, STEP, one, 0)


def pack_weights(source, filled, local, weights, peers):
    return pl.pallas_call(
        pack_weights_kernel,
        out_shape=(
            jax.ShapeDtypeStruct((peers, CAP * PIECE, BLOCK), jnp.bfloat16),
            jax.ShapeDtypeStruct((peers, 1, BLOCK), jnp.int32),
        ),
        grid=(peers // STEP,),
        in_specs=[SMEM(), SMEM(), SMEM(), pl.BlockSpec(weights.shape, lambda i: (0, 0, 0))],
        out_specs=(
            pl.BlockSpec((STEP, CAP * PIECE, BLOCK), lambda i: (i, 0, 0)),
            pl.BlockSpec((STEP, 1, BLOCK), lambda i: (i, 0, 0)),
        ),
        compiler_params=params(),
        name="pack_weights",
    )(source, filled, local, weights)


def slot_weights(pieces, i, s):
    base = s * PIECE
    parts = [pieces[f, i, pl.ds(base, PIECE), :] for f in range(3)]
    parts.append(pieces[3, i, pl.ds(base, 8), :])
    return jnp.concatenate([p.astype(jnp.float32) for p in parts], axis=0).astype(jnp.bfloat16)


def forward_kernel(
    packed, tags, points, arrived, pieces_out, tags_out,
    pieces, tags_in, tags_s, send, buf,
    w_send, w_recv, t_send, t_recv, l_sem, r_send, r_recv, c_send, c_recv, own,
):
    me, feat = lax.axis_index("view"), lax.axis_index("feat")
    peers = packed.shape[0]
    lane = lax.broadcasted_iota(jnp.int32, (GRID, BLOCK), 1)

    own_piece = pltpu.make_async_copy(packed.at[me], pieces.at[feat, me], own.at[0])
    own_piece.start()
    own_tag = pltpu.make_async_copy(tags.at[me], tags_in.at[me], own.at[1])
    own_tag.start()
    greet(me, feat, peers)

    def weights_to(p, at):
        return remote(packed.at[p], pieces.at[feat, at], w_send, w_recv.at[at], p, feat)

    def tags_to(p, at):
        return remote(tags.at[p], tags_in.at[at], t_send, t_recv.at[at], p, feat)

    def relay(q, k):
        return remote(
            pieces.at[feat, q], pieces.at[feat, q], r_send.at[k - 1], r_recv.at[k - 1, q], me, (feat + k) % 4
        )

    def relayed(q, k):
        came = (feat + 4 - k) % 4
        return remote(pieces.at[came, q], pieces.at[came, q], r_send.at[k - 1], r_recv.at[k - 1, q], me, came)

    def tag_copy(q):
        return pltpu.make_async_copy(tags_in.at[q], tags_s.at[q], l_sem.at[q])

    def contrib_to(q):
        return remote(send.at[q], arrived.at[me], c_send, c_recv, q, feat)

    def first(i, carry):
        p = peer_at(me, i, peers)
        tags_to(p, me).start()
        weights_to(p, me).start()
        return carry

    lax.fori_loop(1, peers, first, 0)

    def pass_on(q):
        for k in (1, 3, 2):
            relay(q, k).start()
        tag_copy(q).start()

    def stage_a(i, carry):
        q = peer_at(me, peers - i, peers)
        tags_to(q, q).wait_recv()
        weights_to(q, q).wait_recv()
        pass_on(q)
        return carry

    def product(q):
        for k in (1, 2, 3):
            relayed(q, k).wait_recv()
        tag_copy(q).wait()
        for s in range(CAP):
            block = points[tags_s[q, 0, s]]
            wide = jnp.concatenate([block, block[128:192]], axis=0)
            result = lax.dot_general(slot_weights(pieces, q, s), wide, NT, preferred_element_type=jnp.float32)
            rest = result[:, 128:256]
            buf[s, 0:80, :] = result[:, 0:128]
            buf[s, ROWS : ROWS + GRID, :] = jnp.where(lane < 64, rest[0:GRID], rest[GRID:ROWS])
            buf[s, SLOT - 1 : SLOT, :] = jnp.zeros((1, BLOCK), jnp.float32)
            send[q, pl.ds(s * SLOT, SLOT), :] = buf[s].astype(jnp.bfloat16)

    def stage_b(i, carry):
        product(peer_at(me, peers - i, peers))

        @pl.when(i > 1)
        def _():
            contrib_to(peer_at(me, peers - i + 1, peers)).start()

        return carry

    own_piece.wait()
    own_tag.wait()
    pass_on(me)
    lax.fori_loop(1, LAG, stage_a, 0)

    def both(i, carry):
        stage_a(i, carry)
        return stage_b(i - LAG + 1, carry)

    lax.fori_loop(LAG, peers, both, 0)
    lax.fori_loop(peers - LAG + 1, peers, stage_b, 0)
    product(me)
    contrib_to(peer_at(me, 1, peers)).start()
    keep = pltpu.make_async_copy(pieces, pieces_out, own.at[0])
    keep.start()
    keep_tags = pltpu.make_async_copy(tags_in, tags_out, own.at[1])
    keep_tags.start()
    own_contrib = pltpu.make_async_copy(send.at[me], arrived.at[me], own.at[2])
    own_contrib.start()

    others = pl.ds(0, peers - 1)
    wait_bytes(packed.at[others], w_send)
    wait_bytes(tags.at[others], t_send)
    for k in range(3):
        wait_bytes(packed, r_send.at[k])
    wait_bytes(send.at[others], c_send)
    wait_bytes(send.at[others], c_recv)
    keep.wait()
    keep_tags.wait()
    own_contrib.wait()


def forward_exchange(packed, tags, points):
    peers = packed.shape[0]
    whole = pl.BlockSpec(memory_space=pltpu.VMEM)
    dma = pltpu.SemaphoreType.DMA
    slots = (peers, CAP * SLOT, BLOCK)
    return pl.pallas_call(
        forward_kernel,
        out_shape=(
            jax.ShapeDtypeStruct(slots, jnp.bfloat16),
            jax.ShapeDtypeStruct((4,) + packed.shape, jnp.bfloat16),
            jax.ShapeDtypeStruct(tags.shape, jnp.int32),
        ),
        in_specs=[whole, whole, whole],
        out_specs=(pl.BlockSpec(memory_space=pl.ANY),) * 3,
        scratch_shapes=[
            pltpu.VMEM((4,) + packed.shape, jnp.bfloat16),
            pltpu.VMEM(tags.shape, jnp.int32),
            pltpu.SMEM(tags.shape, jnp.int32),
            pltpu.VMEM(slots, jnp.bfloat16),
            pltpu.VMEM((CAP, SLOT, BLOCK), jnp.float32),
            dma, dma((peers,)), dma, dma((peers,)), dma((peers,)),
            dma((3,)), dma((3, peers)), dma, dma, dma((3,)),
        ],
        compiler_params=params(collective_id=0, has_side_effects=True),
        name="forward_exchange",
    )(packed, tags, points)


def render_kernel(lines, source, line_of, arrived, out, acc):
    step = pl.program_id(0)
    lane = lax.broadcasted_iota(jnp.int32, (GRID, BLOCK), 1)

    @pl.when(step == 0)
    def _():
        acc[...] = jnp.zeros_like(acc)

    def one(i, carry):
        for s in range(CAP):
            at = line_of[source[(step * STEP + i) * CAP + s]] + 1
            acc[at] += arrived[i, pl.ds(s * SLOT, SLOT), :].astype(jnp.float32)
        return carry

    lax.fori_loop(0, STEP, one, 0)

    @pl.when(step == pl.num_programs(0) - 1)
    def _():
        out[...] = jnp.zeros_like(out)
        pairs = pl.ds(ROWS, GRID)

        def finish(k, carry):
            f, m = k // 10, k % 10
            for half in range(2):
                at = f * 20 + half * 10 + m
                out[f, half, m, 0:GRID, :] = (acc[at + 1, 0:GRID, :] + acc[at, GRID:ROWS, :]).astype(jnp.bfloat16)
            low, high = f * 20 + m, f * 20 + 10 + m
            turned = pltpu.roll(jnp.where(lane < 64, acc[high + 1, pairs, :], acc[low, pairs, :]), 64, 1)
            straight = jnp.where(lane < 64, acc[low + 1, pairs, :], acc[high, pairs, :])
            out[f, 2, m, 0:GRID, :] = (turned + straight).astype(jnp.bfloat16)
            return carry

        lax.fori_loop(0, 40, finish, 0)


def render(source, line_of, arrived):
    peers = arrived.shape[0]
    shape = (4, 3, 10, LINE, BLOCK)
    return pl.pallas_call(
        functools.partial(render_kernel, 80),
        out_shape=jax.ShapeDtypeStruct(shape, jnp.bfloat16),
        grid=(peers // STEP,),
        in_specs=[SMEM(), SMEM(), pl.BlockSpec((STEP, CAP * SLOT, BLOCK), lambda i: (i, 0, 0))],
        out_specs=pl.BlockSpec(shape, lambda i: (0, 0, 0, 0, 0)),
        scratch_shapes=[pltpu.VMEM((81, SLOT, BLOCK), jnp.float32)],
        compiler_params=params(),
        name="render",
    )(source, line_of, arrived)


def widened(image, f, lines):
    count = lines * LINE
    lane = lax.broadcasted_iota(jnp.int32, (count, BLOCK), 1)
    pairs = image[f, 2].reshape(count, BLOCK)
    zero = jnp.zeros_like(pairs)
    upper = jnp.concatenate([image[f, 0].reshape(count, BLOCK), jnp.where(lane < 64, pairs, zero)], axis=1)
    lower = jnp.concatenate([image[f, 1].reshape(count, BLOCK), jnp.where(lane < 64, zero, pairs)], axis=1)
    return jnp.concatenate([upper, lower], axis=0)


def compare_kernel(rendered, head, target, grad_image, grad_proj):
    count, width = 2 * LINE, target.shape[-1]
    lane = lax.broadcasted_iota(jnp.int32, (count, BLOCK), 1)
    projected = jnp.zeros((2 * count, width), jnp.float32)
    for f in range(4):
        projected += jnp.dot(widened(rendered, f, 2), head[f], preferred_element_type=jnp.float32)
    scale = jnp.sqrt(jnp.sum(projected * projected, axis=1, keepdims=True) / width + 1e-06)
    inverse = 1.0 / scale
    normed = projected * inverse
    residual = normed - target[...].reshape(2 * count, width).astype(jnp.float32)
    row_dot = jnp.sum(residual * normed, axis=1, keepdims=True) / width
    grad = ((residual - normed * row_dot) * inverse).astype(jnp.bfloat16)
    grad_proj[...] = grad.reshape(grad_proj.shape)
    for f in range(4):
        image = lax.dot_general(grad, head[f], NT, preferred_element_type=jnp.float32)
        for half in range(2):
            grad_image[f, half] = image[half * count : (half + 1) * count, 0:128].astype(jnp.bfloat16).reshape(2, LINE, BLOCK)
        pairs = jnp.where(lane < 64, image[0:count, 128:256], image[count : 2 * count, 128:256])
        grad_image[f, 2] = pairs.astype(jnp.bfloat16).reshape(2, LINE, BLOCK)


def compare(rendered, head, target):
    width = target.shape[-1]
    image = pl.BlockSpec((4, 3, 2, LINE, BLOCK), lambda i: (0, 0, i, 0, 0))
    wide = pl.BlockSpec((2, 2, LINE, width), lambda i: (0, i, 0, 0))
    return pl.pallas_call(
        compare_kernel,
        out_shape=(
            jax.ShapeDtypeStruct(rendered.shape, jnp.bfloat16),
            jax.ShapeDtypeStruct(target.shape, jnp.bfloat16),
        ),
        grid=(5,),
        in_specs=[image, pl.BlockSpec(head.shape, lambda i: (0, 0, 0)), wide],
        out_specs=(image, wide),
        compiler_params=params(),
        name="compare",
    )(rendered, head, target)


def head_kernel(rendered, grad_proj, out):
    rows = widened(rendered, 0, 10)
    for j in range(6):
        grad = grad_proj[:, :, :, j * BLOCK : (j + 1) * BLOCK].reshape(rows.shape[0], BLOCK)
        part = lax.dot_general(rows, grad, TN, preferred_element_type=jnp.float32)
        out[0, j * 6 : j * 6 + 4] = part[0:128].reshape(4, 32, BLOCK)
        out[0, j * 6 + 4 : j * 6 + 6] = (part[128:192] + part[192:256]).reshape(2, 32, BLOCK)


def head_products(rendered, grad_proj):
    rows = 4 * 10 * LINE * 256
    return pl.pallas_call(
        head_kernel,
        out_shape=jax.ShapeDtypeStruct((4, 36, 32, BLOCK), jnp.float32),
        grid=(4,),
        in_specs=[
            pl.BlockSpec((1,) + rendered.shape[1:], lambda i: (i, 0, 0, 0, 0)),
            pl.BlockSpec(grad_proj.shape, lambda i: (0, 0, 0, 0)),
        ],
        out_specs=pl.BlockSpec((1, 36, 32, BLOCK), lambda i: (i, 0, 0, 0)),
        compiler_params=params(),
        name="head_products",
    )(rendered, grad_proj)


def line_slots_kernel(image, slots, buf):
    lane = lax.broadcasted_iota(jnp.int32, (GRID, BLOCK), 1)

    def tail(at):
        return image[at // 20, 2, at % 10, :, :].astype(jnp.float32)[0:GRID]

    def build(k, carry):
        low = k + 1
        low_half = (low // 10) % 2
        own_half = (k // 10) % 2
        own_main = image[k // 20, own_half, k % 10, :, :].astype(jnp.float32)
        low_main = image[low // 20, low_half, low % 10, :, :].astype(jnp.float32)
        buf[0:GRID, :] = own_main[0:GRID]
        buf[GRID:ROWS, :] = low_main[0:GRID]
        own, lower = tail(k), tail(low)
        own = jnp.where(own_half == 0, own, pltpu.roll(own, 64, 1))
        lower = jnp.where(low_half == 1, lower, pltpu.roll(lower, 64, 1))
        buf[ROWS : ROWS + GRID, :] = jnp.where(lane < 64, own, lower)
        slots[k] = buf[...].astype(jnp.bfloat16)
        return carry

    buf[...] = jnp.zeros_like(buf)
    lax.fori_loop(0, slots.shape[0], build, 0)


def line_slots(image, lines):
    whole = pl.BlockSpec(memory_space=pltpu.VMEM)
    return pl.pallas_call(
        line_slots_kernel,
        out_shape=jax.ShapeDtypeStruct((lines, SLOT, BLOCK), jnp.bfloat16),
        in_specs=[whole],
        out_specs=whole,
        scratch_shapes=[pltpu.VMEM((SLOT, BLOCK), jnp.float32)],
        compiler_params=params(),
        name="line_slots",
    )(image)


def backward_kernel(
    source, line_of, slots, head_part, landed, head_out,
    send, head_in, share, share_in, total, total_in,
    g_send, g_recv, x_send, x_recv, a_send, a_recv, b_send, b_recv, own,
):
    me, feat = lax.axis_index("view"), lax.axis_index("feat")
    peers = send.shape[0]
    owners = share.shape[0]
    greet(me, feat, peers)

    def grads_to(p):
        return remote(send.at[p], landed.at[me], g_send, g_recv, p, feat)

    def across(k):
        return remote(head_part.at[(feat + k) % 4], head_in.at[k - 1], x_send.at[k - 1], x_recv.at[k - 1], me, (feat + k) % 4)

    def pack(p):
        for s in range(CAP):
            send[p, pl.ds(s * SLOT, SLOT), :] = slots[line_of[source[p * CAP + s]]]

    def packed_to(i, carry):
        pack(peer_at(me, i, peers))

        @pl.when(i > 1)
        def _():
            grads_to(peer_at(me, i - 1, peers)).start()

        return carry

    for k in (1, 3, 2):
        across(k).start()
    middle = peers // 2
    lax.fori_loop(1, middle, packed_to, 0)

    for k in (1, 2, 3):
        across(k).wait_recv()

    def add(t, carry):
        value = head_part[feat, t] + head_in[0, t] + head_in[1, t] + head_in[2, t]
        share[t] = value.astype(jnp.bfloat16)
        return carry

    lax.fori_loop(0, owners, add, 0)
    lax.fori_loop(middle, middle + 4, packed_to, 0)

    def share_to(p):
        return remote(share.at[p], share_in.at[me], a_send.at[p], a_recv, p, feat)

    def give(i, carry):
        p = peer_at(me, i, peers)

        @pl.when(p < owners)
        def _():
            share_to(p).start()

        return carry

    lax.fori_loop(1, peers, give, 0)
    lax.fori_loop(middle + 4, peers, packed_to, 0)
    pack(me)
    grads_to(peer_at(me, peers - 1, peers)).start()
    own_grads = pltpu.make_async_copy(send.at[me], landed.at[me], own.at[0])
    own_grads.start()
    others = pl.ds(0, peers - 1)

    def total_to(p, at):
        return remote(total, total_in.at[at], b_send, b_recv.at[at], p, feat)

    @pl.when(me < owners)
    def _():
        mine = pltpu.make_async_copy(share.at[me], share_in.at[me], own.at[1])
        mine.start()
        mine.wait()
        wait_bytes(share_in.at[others], a_recv)

        def gather(q, value):
            return value + share_in[q].astype(jnp.float32)

        value = lax.fori_loop(0, peers, gather, jnp.zeros(total.shape, jnp.float32))
        total[...] = value.astype(jnp.bfloat16)
        kept = pltpu.make_async_copy(total, total_in.at[me], own.at[1])
        kept.start()
        kept.wait()

        def tell(i, carry):
            total_to(peer_at(me, i, peers), me).start()
            return carry

        lax.fori_loop(1, peers, tell, 0)
        wait_bytes(share_in.at[others], b_send)

    def sent(i, carry):
        p = peer_at(me, i, peers)

        @pl.when(p < owners)
        def _():
            share_to(p).wait_send()
            total_to(p, p).wait_recv()

        return carry

    lax.fori_loop(1, peers, sent, 0)
    result = pltpu.make_async_copy(total_in, head_out, own.at[1])
    result.start()
    for k in (1, 2, 3):
        across(k).wait_send()
    wait_bytes(send.at[others], g_send)
    wait_bytes(send.at[others], g_recv)
    own_grads.wait()
    result.wait()


def backward_exchange(source, line_of, slots, head_part, peers):
    whole = pl.BlockSpec(memory_space=pltpu.VMEM)
    dma = pltpu.SemaphoreType.DMA
    owners = head_part.shape[1]
    tile = head_part.shape[2:]
    shape = (peers, CAP * SLOT, BLOCK)
    return pl.pallas_call(
        backward_kernel,
        out_shape=(
            jax.ShapeDtypeStruct(shape, jnp.bfloat16),
            jax.ShapeDtypeStruct((owners,) + tile, jnp.bfloat16),
        ),
        in_specs=[SMEM(), SMEM(), whole, whole],
        out_specs=(pl.BlockSpec(memory_space=pl.ANY),) * 2,
        scratch_shapes=[
            pltpu.VMEM(shape, jnp.bfloat16),
            pltpu.VMEM((3, owners) + tile, jnp.float32),
            pltpu.VMEM((owners,) + tile, jnp.bfloat16),
            pltpu.VMEM((peers,) + tile, jnp.bfloat16),
            pltpu.VMEM(tile, jnp.bfloat16),
            pltpu.VMEM((owners,) + tile, jnp.bfloat16),
            dma, dma, dma((3,)), dma((3,)), dma((owners,)), dma, dma, dma((owners,)), dma((2,)),
        ],
        compiler_params=params(collective_id=1, has_side_effects=True),
        name="backward_exchange",
    )(source, line_of, slots, head_part)


def unsplat_kernel(ids, pieces, arrived, out, acc):
    step = pl.program_id(0)
    lane = lax.broadcasted_iota(jnp.int32, (GRID, BLOCK), 1)

    @pl.when(step == 0)
    def _():
        acc[...] = jnp.zeros_like(acc)

    def one(i, carry):
        for s in range(CAP):
            at = ids[(step * STEP + i) * CAP + s]
            weights = slot_weights(pieces, i, s)
            slot = arrived[i, pl.ds(s * SLOT, SLOT), :].astype(jnp.float32)
            pair = slot[ROWS : ROWS + GRID]
            rest = jnp.concatenate(
                [jnp.where(lane < 64, pair, 0.0), jnp.where(lane < 64, 0.0, pair), jnp.zeros((6, BLOCK), jnp.float32)], axis=0
            )
            both = jnp.concatenate([slot[0:80], rest], axis=1).astype(jnp.bfloat16)
            product = lax.dot_general(both, weights, TN, preferred_element_type=jnp.float32)
            acc[at, 0:128, :] += product[0:128].astype(jnp.bfloat16).astype(jnp.float32)
            acc[at, 128:192, :] += (product[128:192] + product[192:256]).astype(jnp.bfloat16).astype(jnp.float32)
        return carry

    lax.fori_loop(0, STEP, one, 0)

    @pl.when(step == pl.num_programs(0) - 1)
    def _():
        out[...] = acc[...].astype(jnp.bfloat16)


def unsplat(ids, pieces, arrived, shape):
    peers = arrived.shape[0]
    return pl.pallas_call(
        unsplat_kernel,
        out_shape=jax.ShapeDtypeStruct(shape, jnp.bfloat16),
        grid=(peers // STEP,),
        in_specs=[
            SMEM(),
            pl.BlockSpec((4, STEP, CAP * PIECE, BLOCK), lambda i: (0, i, 0, 0)),
            pl.BlockSpec((STEP, CAP * SLOT, BLOCK), lambda i: (i, 0, 0)),
        ],
        out_specs=pl.BlockSpec(shape, lambda i: (0, 0, 0)),
        scratch_shapes=[pltpu.VMEM(shape, jnp.float32)],
        compiler_params=params(),
        name="unsplat",
    )(ids, pieces, arrived)


def per_device(points, head_weight, teacher, splat_weight, block_owner, block_local, block_row):
    peers = lax.axis_size("view")
    feat = lax.axis_index("feat")
    local_width = points.shape[1]
    views, visible = splat_weight.shape[:2]
    requests = views * visible
    lines = views * GRID
    rows = 20 * LINE

    source, filled = slot_plan(block_owner.reshape(requests), peers, CAP)
    local = block_local.reshape(requests)
    line_of = (block_row + jnp.arange(views, dtype=jnp.int32)[:, None] * GRID).reshape(requests)

    mine = lax.dynamic_slice_in_dim(
        jnp.pad(splat_weight, ((0, 0), (0, 0), (0, 4 * PIECE - ROWS), (0, 0))), feat * PIECE, PIECE, axis=2
    ).reshape(requests, PIECE, BLOCK)
    packed, tags = pack_weights(source, filled, local, mine, peers)

    head = lax.all_gather(head_weight, "feat", axis=0)
    head = jnp.concatenate([head, head[:, 128:192]], axis=1)
    wanted = jnp.pad(
        teacher.reshape(local_width, lines, GRID), ((0, 0), (0, 80 - lines), (0, LINE - GRID))
    ).reshape(local_width, 4, rows)
    target = lax.all_to_all(wanted.transpose(1, 0, 2), "feat", split_axis=0, concat_axis=0, tiled=True)
    target = target.reshape(4 * local_width, rows).T.reshape(2, 10, LINE, 4 * local_width)

    arrived, pieces, tags_in = forward_exchange(packed, tags, points)
    ids = tags_in[:, 0, :CAP].reshape(peers * CAP)
    image = render(source, line_of, arrived)
    rendered = lax.all_to_all(image, "feat", split_axis=0, concat_axis=0, tiled=True)
    grad_image, grad_proj = compare(rendered, head, target)
    grad_rows = lax.all_to_all(grad_image, "feat", split_axis=0, concat_axis=0, tiled=True)
    head_part = head_products(rendered, grad_proj)
    slots = line_slots(grad_rows, lines)
    landed, head_sum = backward_exchange(source, line_of, slots, head_part, peers)
    grad_points = unsplat(ids, pieces, landed, points.shape)
    head_grad = head_sum.reshape(6, local_width, BLOCK).transpose(1, 0, 2).reshape(local_width, 6 * BLOCK)
    return grad_points, head_grad.astype(jnp.float32) / (views * peers * GRID)


def solution(mesh):
    placed = (
        P("view", "feat", None),
        P("feat", None),
        P("feat", "view", None),
        P("view", None, None, None),
        P("view", None, None),
        P("view", None),
        P("view", None),
    )
    return jax.shard_map(
        per_device,
        mesh=mesh,
        in_specs=placed,
        out_specs=(P("view", "feat", None), P("feat", None)),
        check_vma=False,
    )
```

```python
import functools

import jax
import jax.numpy as jnp
from jax import lax
from jax.experimental import pallas as pl
from jax.experimental.pallas import tpu as pltpu
from jax.sharding import PartitionSpec as P

GRID = 37
BAND = 2
BLOCK = 128
CAP = 3
ROWS = BAND * GRID
PIECE = 24
SLOT = 112
LINE = 40
STEP = 8
STRIDE = 27
LAG = 12
MESH = pl.DeviceIdType.MESH
SMEM = functools.partial(pl.BlockSpec, memory_space=pltpu.SMEM)
NT = (((1,), (1,)), ((), ()))
TN = (((0,), (0,)), ((), ()))
VMEM_LIMIT = 60 * 1024 * 1024


def params(**kw):
    return pltpu.CompilerParams(vmem_limit_bytes=VMEM_LIMIT, **kw)


def slot_plan(owners, peer_count, capacity):
    total_requests = owners.shape[0]
    positions = jnp.arange(total_requests, dtype=jnp.int32)
    earlier = (owners[:, None] == owners[None, :]) & (positions[None, :] < positions[:, None])
    slot_rank = jnp.sum(earlier.astype(jnp.int32), axis=1)
    target = owners * capacity + slot_rank
    slot_ids = jnp.arange(peer_count * capacity, dtype=jnp.int32)
    matches = target[None, :] == slot_ids[:, None]
    source = jnp.sum(jnp.where(matches, positions[None, :], 0), axis=1)
    filled = jnp.any(matches, axis=1)
    return source, filled.astype(jnp.int32)


def peer_at(me, i, peers):
    return (me + i * STRIDE) % peers


def greet(me, feat, peers):
    barrier = pltpu.get_barrier_semaphore()

    def hello(i, carry):
        pl.semaphore_signal(barrier, inc=1, device_id=(peer_at(me, i, peers), feat), device_id_type=MESH)
        return carry

    lax.fori_loop(1, peers, hello, 0)
    for k in range(1, 4):
        pl.semaphore_signal(barrier, inc=1, device_id=(me, (feat + k) % 4), device_id_type=MESH)
    pl.semaphore_wait(barrier, peers + 2)


def remote(src, dst, send, recv, view, feat):
    return pltpu.make_async_remote_copy(
        src_ref=src, dst_ref=dst, send_sem=send, recv_sem=recv, device_id=(view, feat), device_id_type=MESH
    )


def wait_bytes(ref, sem):
    pltpu.make_async_copy(ref, ref, sem).wait()


def pack_weights_kernel(source, filled, local, weights, out, tags):
    step = pl.program_id(0)
    lane = lax.broadcasted_iota(jnp.int32, (1, BLOCK), 1)

    def one(i, carry):
        tag = jnp.zeros((1, BLOCK), jnp.int32)
        for s in range(CAP):
            t = (step * STEP + i) * CAP + s
            src = source[t]
            piece = jnp.where(filled[t] > 0, weights[src].astype(jnp.float32), 0.0)
            out[i, pl.ds(s * PIECE, PIECE), :] = piece.astype(jnp.bfloat16)
            tag = jnp.where(lane == s, local[src], tag)
        tags[i] = tag
        return carry

    lax.fori_loop(0, STEP, one, 0)


def pack_weights(source, filled, local, weights, peers):
    return pl.pallas_call(
        pack_weights_kernel,
        out_shape=(
            jax.ShapeDtypeStruct((peers, CAP * PIECE, BLOCK), jnp.bfloat16),
            jax.ShapeDtypeStruct((peers, 1, BLOCK), jnp.int32),
        ),
        grid=(peers // STEP,),
        in_specs=[SMEM(), SMEM(), SMEM(), pl.BlockSpec(weights.shape, lambda i: (0, 0, 0))],
        out_specs=(
            pl.BlockSpec((STEP, CAP * PIECE, BLOCK), lambda i: (i, 0, 0)),
            pl.BlockSpec((STEP, 1, BLOCK), lambda i: (i, 0, 0)),
        ),
        compiler_params=params(),
        name="pack_weights",
    )(source, filled, local, weights)


def slot_weights(pieces, i, s):
    base = s * PIECE
    parts = [pieces[f, i, pl.ds(base, PIECE), :] for f in range(3)]
    parts.append(pieces[3, i, pl.ds(base, 8), :])
    return jnp.concatenate([p.astype(jnp.float32) for p in parts], axis=0).astype(jnp.bfloat16)


def forward_kernel(
    packed, tags, points, head, wanted, arrived, pieces_out, tags_out, head_out, target,
    pieces, tags_in, tags_s, send, buf, head_in, head_turned,
    w_send, w_recv, t_send, t_recv, l_sem, r_send, r_recv, c_send, c_recv, h_send, h_recv, y_send, y_recv, own,
):
    me, feat = lax.axis_index("view"), lax.axis_index("feat")
    peers = packed.shape[0]
    lane = lax.broadcasted_iota(jnp.int32, (GRID, BLOCK), 1)

    own_piece = pltpu.make_async_copy(packed.at[me], pieces.at[feat, me], own.at[0])
    own_piece.start()
    own_tag = pltpu.make_async_copy(tags.at[me], tags_in.at[me], own.at[1])
    own_tag.start()
    greet(me, feat, peers)

    def weights_to(p, at):
        return remote(packed.at[p], pieces.at[feat, at], w_send, w_recv.at[at], p, feat)

    def tags_to(p, at):
        return remote(tags.at[p], tags_in.at[at], t_send, t_recv.at[at], p, feat)

    def relay(q, k):
        return remote(
            pieces.at[feat, q], pieces.at[feat, q], r_send.at[k - 1], r_recv.at[k - 1, q], me, (feat + k) % 4
        )

    def relayed(q, k):
        came = (feat + 4 - k) % 4
        return remote(pieces.at[came, q], pieces.at[came, q], r_send.at[k - 1], r_recv.at[k - 1, q], me, came)

    def tag_copy(q):
        return pltpu.make_async_copy(tags_in.at[q], tags_s.at[q], l_sem.at[q])

    def contrib_to(q):
        return remote(send.at[q], arrived.at[me], c_send, c_recv, q, feat)

    def first(i, carry):
        p = peer_at(me, i, peers)
        tags_to(p, me).start()
        weights_to(p, me).start()
        return carry

    lax.fori_loop(1, peers, first, 0)

    def pass_on(q):
        for k in (1, 3, 2):
            relay(q, k).start()
        tag_copy(q).start()

    def stage_a(i, carry):
        q = peer_at(me, peers - i, peers)
        tags_to(q, q).wait_recv()
        weights_to(q, q).wait_recv()
        pass_on(q)
        return carry

    def product(q):
        for k in (1, 2, 3):
            relayed(q, k).wait_recv()
        tag_copy(q).wait()
        for s in range(CAP):
            block = points[tags_s[q, 0, s]]
            wide = jnp.concatenate([block, block[128:192]], axis=0)
            result = lax.dot_general(slot_weights(pieces, q, s), wide, NT, preferred_element_type=jnp.float32)
            rest = result[:, 128:256]
            buf[s, 0:80, :] = result[:, 0:128]
            buf[s, ROWS : ROWS + GRID, :] = jnp.where(lane < 64, rest[0:GRID], rest[GRID:ROWS])
            buf[s, SLOT - 1 : SLOT, :] = jnp.zeros((1, BLOCK), jnp.float32)
            send[q, pl.ds(s * SLOT, SLOT), :] = buf[s].astype(jnp.bfloat16)

    def stage_b(i, carry):
        product(peer_at(me, peers - i, peers))

        @pl.when(i > 1)
        def _():
            contrib_to(peer_at(me, peers - i + 1, peers)).start()

        return carry

    own_piece.wait()
    own_tag.wait()
    pass_on(me)
    lax.fori_loop(1, LAG, stage_a, 0)

    def both(i, carry):
        stage_a(i, carry)
        return stage_b(i - LAG + 1, carry)

    lax.fori_loop(LAG, peers, both, 0)
    lax.fori_loop(peers - LAG + 1, peers, stage_b, 0)

    def head_to(k):
        return remote(head, head_in.at[feat], h_send.at[k - 1], h_recv.at[k - 1], me, (feat + k) % 4)

    def wanted_to(k):
        dst = (feat + k) % 4
        return remote(wanted.at[dst], target.at[feat], y_send.at[k - 1], y_recv.at[k - 1], me, dst)

    for k in (1, 3, 2):
        head_to(k).start()
    for k in (1, 3, 2):
        wanted_to(k).start()
    own_head = pltpu.make_async_copy(head, head_in.at[feat], own.at[3])
    own_head.start()
    own_wanted = pltpu.make_async_copy(wanted.at[feat], target.at[feat], own.at[4])
    own_wanted.start()
    product(me)
    contrib_to(peer_at(me, 1, peers)).start()
    keep = pltpu.make_async_copy(pieces, pieces_out, own.at[0])
    keep.start()
    keep_tags = pltpu.make_async_copy(tags_in, tags_out, own.at[1])
    keep_tags.start()
    own_contrib = pltpu.make_async_copy(send.at[me], arrived.at[me], own.at[2])
    own_contrib.start()

    own_head.wait()
    for k in (1, 2, 3):
        head_to(k).wait_recv()

    def turn(f, carry):
        full = head_in[f].astype(jnp.float32)
        mains = [full[:, 192 * c : 192 * c + 128] for c in range(4)]
        tails = [full[:, 192 * c + 128 : 192 * c + 192] for c in range(4)]
        head_turned[f] = jnp.concatenate(mains + tails, axis=1).astype(jnp.bfloat16)
        return carry

    lax.fori_loop(0, 4, turn, 0)
    own_wanted.wait()
    for k in (1, 2, 3):
        head_to(k).wait_send()
        wanted_to(k).wait_send()
        wanted_to(k).wait_recv()
    others = pl.ds(0, peers - 1)
    keep_head = pltpu.make_async_copy(head_turned, head_out, own.at[3])
    keep_head.start()
    wait_bytes(packed.at[others], w_send)
    wait_bytes(tags.at[others], t_send)
    for k in range(3):
        wait_bytes(packed, r_send.at[k])
    wait_bytes(send.at[others], c_send)
    wait_bytes(send.at[others], c_recv)
    keep.wait()
    keep_tags.wait()
    own_contrib.wait()
    keep_head.wait()


def forward_exchange(packed, tags, points, head, wanted):
    peers = packed.shape[0]
    whole = pl.BlockSpec(memory_space=pltpu.VMEM)
    dma = pltpu.SemaphoreType.DMA
    slots = (peers, CAP * SLOT, BLOCK)
    return pl.pallas_call(
        forward_kernel,
        out_shape=(
            jax.ShapeDtypeStruct(slots, jnp.bfloat16),
            jax.ShapeDtypeStruct((4,) + packed.shape, jnp.bfloat16),
            jax.ShapeDtypeStruct(tags.shape, jnp.int32),
            jax.ShapeDtypeStruct((4,) + head.shape, jnp.bfloat16),
            jax.ShapeDtypeStruct(wanted.shape, jnp.bfloat16),
        ),
        in_specs=[whole] * 5,
        out_specs=(pl.BlockSpec(memory_space=pl.ANY),) * 5,
        scratch_shapes=[
            pltpu.VMEM((4,) + packed.shape, jnp.bfloat16),
            pltpu.VMEM(tags.shape, jnp.int32),
            pltpu.SMEM(tags.shape, jnp.int32),
            pltpu.VMEM(slots, jnp.bfloat16),
            pltpu.VMEM((CAP, SLOT, BLOCK), jnp.float32),
            pltpu.VMEM((4,) + head.shape, jnp.bfloat16),
            pltpu.VMEM((4,) + head.shape, jnp.bfloat16),
            dma, dma((peers,)), dma, dma((peers,)), dma((peers,)),
            dma((3,)), dma((3, peers)), dma, dma,
            dma((3,)), dma((3,)), dma((3,)), dma((3,)), dma((5,)),
        ],
        compiler_params=params(collective_id=0, has_side_effects=True),
        name="forward_exchange",
    )(packed, tags, points, head, wanted)


def render_kernel(lines, source, line_of, arrived, out, acc):
    step = pl.program_id(0)
    lane = lax.broadcasted_iota(jnp.int32, (GRID, BLOCK), 1)

    @pl.when(step == 0)
    def _():
        acc[...] = jnp.zeros_like(acc)

    def one(i, carry):
        for s in range(CAP):
            at = line_of[source[(step * STEP + i) * CAP + s]] + 1
            acc[at] += arrived[i, pl.ds(s * SLOT, SLOT), :].astype(jnp.float32)
        return carry

    lax.fori_loop(0, STEP, one, 0)

    @pl.when(step == pl.num_programs(0) - 1)
    def _():
        out[...] = jnp.zeros_like(out)
        pairs = pl.ds(ROWS, GRID)

        def finish(k, carry):
            f, m = k // 10, k % 10
            for half in range(2):
                at = f * 20 + half * 10 + m
                out[f, half, m, 0:GRID, :] = (acc[at + 1, 0:GRID, :] + acc[at, GRID:ROWS, :]).astype(jnp.bfloat16)
            low, high = f * 20 + m, f * 20 + 10 + m
            turned = pltpu.roll(jnp.where(lane < 64, acc[high + 1, pairs, :], acc[low, pairs, :]), 64, 1)
            straight = jnp.where(lane < 64, acc[low + 1, pairs, :], acc[high, pairs, :])
            out[f, 2, m, 0:GRID, :] = (turned + straight).astype(jnp.bfloat16)
            return carry

        lax.fori_loop(0, 40, finish, 0)


def render(source, line_of, arrived):
    peers = arrived.shape[0]
    shape = (4, 3, 10, LINE, BLOCK)
    return pl.pallas_call(
        functools.partial(render_kernel, 80),
        out_shape=jax.ShapeDtypeStruct(shape, jnp.bfloat16),
        grid=(peers // STEP,),
        in_specs=[SMEM(), SMEM(), pl.BlockSpec((STEP, CAP * SLOT, BLOCK), lambda i: (i, 0, 0))],
        out_specs=pl.BlockSpec(shape, lambda i: (0, 0, 0, 0, 0)),
        scratch_shapes=[pltpu.VMEM((81, SLOT, BLOCK), jnp.float32)],
        compiler_params=params(),
        name="render",
    )(source, line_of, arrived)


def widened(image, f, start, lines):
    count = lines * LINE
    lane = lax.broadcasted_iota(jnp.int32, (count, BLOCK), 1)
    parts = [image[f, j, pl.ds(start, lines)].reshape(count, BLOCK) for j in range(3)]
    zero = jnp.zeros_like(parts[2])
    upper = jnp.concatenate([parts[0], jnp.where(lane < 64, parts[2], zero)], axis=1)
    lower = jnp.concatenate([parts[1], jnp.where(lane < 64, zero, parts[2])], axis=1)
    return jnp.concatenate([upper, lower], axis=0)


def target_rows(target, start, lines):
    count = lines * LINE
    lane = lax.broadcasted_iota(jnp.int32, (count, BLOCK), 1)
    part = [
        [target[f, j, pl.ds(start, lines)].reshape(count, BLOCK).astype(jnp.float32) for j in range(3)] for f in range(4)
    ]
    halves = []
    for half in range(2):
        row = [part[f][half] for f in range(4)]
        for f in (0, 2):
            first, second = part[f][2], part[f + 1][2]
            if half == 0:
                second = pltpu.roll(second, 64, 1)
            else:
                first = pltpu.roll(first, 64, 1)
            row.append(jnp.where(lane < 64, first, second))
        halves.append(jnp.concatenate(row, axis=1))
    return jnp.concatenate(halves, axis=0)


def doubled(head, f):
    full = head[f]
    return jnp.concatenate([full, full[128:192]], axis=0)


def compare_chunk(g, rendered, head, target, grad_image, grad_proj):
    count, width = 2 * LINE, head.shape[-1]
    lane = lax.broadcasted_iota(jnp.int32, (count, BLOCK), 1)
    projected = jnp.zeros((2 * count, width), jnp.float32)
    for f in range(4):
        projected += jnp.dot(widened(rendered, f, 2 * g, 2), doubled(head, f), preferred_element_type=jnp.float32)
    scale = jnp.sqrt(jnp.sum(projected * projected, axis=1, keepdims=True) / width + 1e-06)
    inverse = 1.0 / scale
    normed = projected * inverse
    residual = normed - target_rows(target, 2 * g, 2)
    row_dot = jnp.sum(residual * normed, axis=1, keepdims=True) / width
    grad = ((residual - normed * row_dot) * inverse).astype(jnp.bfloat16)
    grad_proj[:, pl.ds(2 * g, 2)] = grad.reshape(2, 2, LINE, width)
    for f in range(4):
        image = lax.dot_general(grad, doubled(head, f), NT, preferred_element_type=jnp.float32)
        for half in range(2):
            main = image[half * count : (half + 1) * count, 0:128]
            grad_image[f, half, pl.ds(2 * g, 2)] = main.astype(jnp.bfloat16).reshape(2, LINE, BLOCK)
        pairs = jnp.where(lane < 64, image[0:count, 128:256], image[count : 2 * count, 128:256])
        grad_image[f, 2, pl.ds(2 * g, 2)] = pairs.astype(jnp.bfloat16).reshape(2, LINE, BLOCK)


def head_product(f, rendered, grad_proj, out):
    rows = widened(rendered, f, 0, 10)
    for j in range(3):
        grad = grad_proj[:, :, :, j * 256 : (j + 1) * 256].reshape(rows.shape[0], 256)
        part = lax.dot_general(rows, grad, TN, preferred_element_type=jnp.float32)
        for h in range(2):
            base, cols = j * 12 + h * 6, part[:, h * 128 : (h + 1) * 128]
            out[f, base : base + 4] = cols[0:128].reshape(4, 32, BLOCK)
            out[f, base + 4 : base + 6] = (cols[128:192] + cols[192:256]).reshape(2, 32, BLOCK)


def build_slots(image, slots, buf):
    lane = lax.broadcasted_iota(jnp.int32, (GRID, BLOCK), 1)

    def tail(at):
        return image[at // 20, 2, at % 10, :, :].astype(jnp.float32)[0:GRID]

    def build(k, carry):
        low = k + 1
        low_half = (low // 10) % 2
        own_half = (k // 10) % 2
        own_main = image[k // 20, own_half, k % 10, :, :].astype(jnp.float32)
        low_main = image[low // 20, low_half, low % 10, :, :].astype(jnp.float32)
        slot = k % 2
        buf[slot, 0:GRID, :] = own_main[0:GRID]
        buf[slot, GRID:ROWS, :] = low_main[0:GRID]
        own, lower = tail(k), tail(low)
        own = jnp.where(own_half == 0, own, pltpu.roll(own, 64, 1))
        lower = jnp.where(low_half == 1, lower, pltpu.roll(lower, 64, 1))
        buf[slot, ROWS : ROWS + GRID, :] = jnp.where(lane < 64, own, lower)
        slots[k] = buf[slot].astype(jnp.bfloat16)
        return carry

    buf[...] = jnp.zeros_like(buf)
    lax.fori_loop(0, slots.shape[0], build, 0)


def backward_kernel(
    source, line_of, image, head, target, landed, head_out,
    rendered, grad_image, grad_in, grad_proj, head_part, slots, buf,
    send, head_in, share, share_in, total, total_in,
    p_send, p_recv, q_send, q_recv,
    g_send, g_recv, x_send, x_recv, a_send, a_recv, b_send, b_recv, own,
):
    me, feat = lax.axis_index("view"), lax.axis_index("feat")
    peers = send.shape[0]
    owners = share.shape[0]
    own_image = pltpu.make_async_copy(image.at[feat], rendered.at[feat], own.at[0])
    own_image.start()
    greet(me, feat, peers)

    def image_to(k, g):
        dst, chunk = (feat + k) % 4, pl.ds(2 * g, 2)
        return remote(
            image.at[dst, :, chunk], rendered.at[feat, :, chunk], p_send.at[k - 1, g], p_recv.at[k - 1, g], me, dst
        )

    def grads_back(k, g):
        dst, chunk = (feat + k) % 4, pl.ds(2 * g, 2)
        return remote(
            grad_image.at[dst, :, chunk], grad_in.at[feat, :, chunk], q_send.at[k - 1, g], q_recv.at[k - 1, g], me, dst
        )

    def hand_out(g, carry):
        for k in (1, 3, 2):
            image_to(k, g).start()
        return carry

    lax.fori_loop(0, 5, hand_out, 0)
    own_image.wait()

    def chunk_step(g, carry):
        for k in (1, 2, 3):
            image_to(k, g).wait_recv()
        compare_chunk(g, rendered, head, target, grad_image, grad_proj)

        @pl.when(g > 0)
        def _():
            for k in (1, 3, 2):
                grads_back(k, g - 1).start()

        return carry

    lax.fori_loop(0, 5, chunk_step, 0)
    head_product(0, rendered, grad_proj, head_part)
    for k in (1, 3, 2):
        grads_back(k, 4).start()
    own_back = pltpu.make_async_copy(grad_image.at[feat], grad_in.at[feat], own.at[0])
    own_back.start()

    def head_step(f, carry):
        head_product(f, rendered, grad_proj, head_part)
        return carry

    lax.fori_loop(1, 4, head_step, 0)

    def across(k):
        return remote(head_part.at[(feat + k) % 4], head_in.at[k - 1], x_send.at[k - 1], x_recv.at[k - 1], me, (feat + k) % 4)

    for k in (1, 3, 2):
        across(k).start()

    def returned(g, carry):
        for k in (1, 2, 3):
            grads_back(k, g).wait_recv()
        return carry

    lax.fori_loop(0, 5, returned, 0)
    own_back.wait()
    build_slots(grad_in, slots, buf)

    def grads_to(p):
        return remote(send.at[p], landed.at[me], g_send, g_recv, p, feat)

    def pack(p):
        for s in range(CAP):
            send[p, pl.ds(s * SLOT, SLOT), :] = slots[line_of[source[p * CAP + s]]]

    def packed_to(i, carry):
        pack(peer_at(me, i, peers))

        @pl.when(i > 1)
        def _():
            grads_to(peer_at(me, i - 1, peers)).start()

        return carry

    early, late = peers * 3 // 8, peers * 3 // 4
    lax.fori_loop(1, early, packed_to, 0)
    for k in (1, 2, 3):
        across(k).wait_recv()

    def add(t, carry):
        value = head_part[feat, t] + head_in[0, t] + head_in[1, t] + head_in[2, t]
        share[t] = value.astype(jnp.bfloat16)
        return carry

    lax.fori_loop(0, owners, add, 0)
    lax.fori_loop(early, early + 2, packed_to, 0)

    def share_to(p):
        return remote(share.at[p], share_in.at[me], a_send.at[p], a_recv, p, feat)

    def give(i, carry):
        p = peer_at(me, i, peers)

        @pl.when(p < owners)
        def _():
            share_to(p).start()

        return carry

    lax.fori_loop(1, peers, give, 0)
    lax.fori_loop(early + 2, late, packed_to, 0)
    others = pl.ds(0, peers - 1)

    def total_to(p, at):
        return remote(total, total_in.at[at], b_send, b_recv.at[at], p, feat)

    @pl.when(me < owners)
    def _():
        mine = pltpu.make_async_copy(share.at[me], share_in.at[me], own.at[1])
        mine.start()
        mine.wait()
        wait_bytes(share_in.at[others], a_recv)

        def gather(q, value):
            return value + share_in[q].astype(jnp.float32)

        value = lax.fori_loop(0, peers, gather, jnp.zeros(total.shape, jnp.float32))
        total[...] = value.astype(jnp.bfloat16)
        kept = pltpu.make_async_copy(total, total_in.at[me], own.at[1])
        kept.start()
        kept.wait()

        def tell(i, carry):
            total_to(peer_at(me, i, peers), me).start()
            return carry

        lax.fori_loop(1, peers, tell, 0)

    lax.fori_loop(late, peers, packed_to, 0)
    pack(me)
    grads_to(peer_at(me, peers - 1, peers)).start()
    own_grads = pltpu.make_async_copy(send.at[me], landed.at[me], own.at[0])
    own_grads.start()

    @pl.when(me < owners)
    def _():
        wait_bytes(share_in.at[others], b_send)

    def sent(i, carry):
        p = peer_at(me, i, peers)

        @pl.when(p < owners)
        def _():
            share_to(p).wait_send()
            total_to(p, p).wait_recv()

        return carry

    lax.fori_loop(1, peers, sent, 0)
    result = pltpu.make_async_copy(total_in, head_out, own.at[1])
    result.start()

    def drain(g, carry):
        for k in (1, 2, 3):
            image_to(k, g).wait_send()
            grads_back(k, g).wait_send()
        return carry

    lax.fori_loop(0, 5, drain, 0)
    for k in (1, 2, 3):
        across(k).wait_send()
    wait_bytes(send.at[others], g_send)
    wait_bytes(send.at[others], g_recv)
    own_grads.wait()
    result.wait()


def backward_exchange(source, line_of, image, head, target, lines, peers):
    whole = pl.BlockSpec(memory_space=pltpu.VMEM)
    dma = pltpu.SemaphoreType.DMA
    owners, tile = 36, (32, BLOCK)
    shape = (peers, CAP * SLOT, BLOCK)
    return pl.pallas_call(
        backward_kernel,
        out_shape=(
            jax.ShapeDtypeStruct(shape, jnp.bfloat16),
            jax.ShapeDtypeStruct((owners,) + tile, jnp.bfloat16),
        ),
        in_specs=[SMEM(), SMEM(), whole, whole, whole],
        out_specs=(pl.BlockSpec(memory_space=pl.ANY),) * 2,
        scratch_shapes=[
            pltpu.VMEM(image.shape, jnp.bfloat16),
            pltpu.VMEM(image.shape, jnp.bfloat16),
            pltpu.VMEM(image.shape, jnp.bfloat16),
            pltpu.VMEM((2, 10, LINE, head.shape[-1]), jnp.bfloat16),
            pltpu.VMEM((4, owners) + tile, jnp.float32),
            pltpu.VMEM((lines, SLOT, BLOCK), jnp.bfloat16),
            pltpu.VMEM((2, SLOT, BLOCK), jnp.float32),
            pltpu.VMEM(shape, jnp.bfloat16),
            pltpu.VMEM((3, owners) + tile, jnp.float32),
            pltpu.VMEM((owners,) + tile, jnp.bfloat16),
            pltpu.VMEM((peers,) + tile, jnp.bfloat16),
            pltpu.VMEM(tile, jnp.bfloat16),
            pltpu.VMEM((owners,) + tile, jnp.bfloat16),
            dma((3, 5)), dma((3, 5)), dma((3, 5)), dma((3, 5)),
            dma, dma, dma((3,)), dma((3,)), dma((owners,)), dma, dma, dma((owners,)), dma((2,)),
        ],
        compiler_params=params(collective_id=1, has_side_effects=True),
        name="backward_exchange",
    )(source, line_of, image, head, target)


def unsplat_kernel(ids, pieces, arrived, out, acc, products):
    step = pl.program_id(0)
    lane = lax.broadcasted_iota(jnp.int32, (GRID, BLOCK), 1)

    @pl.when(step == 0)
    def _():
        acc[...] = jnp.zeros_like(acc)

    def product(i, s):
        slot = arrived[i, pl.ds(s * SLOT, SLOT), :].astype(jnp.float32)
        pair = slot[ROWS : ROWS + GRID]
        rest = jnp.concatenate(
            [jnp.where(lane < 64, pair, 0.0), jnp.where(lane < 64, 0.0, pair), jnp.zeros((6, BLOCK), jnp.float32)], axis=0
        )
        both = jnp.concatenate([slot[0:80], rest], axis=1).astype(jnp.bfloat16)
        return lax.dot_general(both, slot_weights(pieces, i, s), TN, preferred_element_type=jnp.float32)

    def one(i, carry):
        for n in range(2):
            for s in range(CAP):
                result = product(2 * i + n, s)
                products[n * CAP + s, 0:128, :] = result[0:128]
                products[n * CAP + s, 128:192, :] = result[128:192] + result[192:256]
        for n in range(2):
            for s in range(CAP):
                at = ids[(step * STEP + 2 * i + n) * CAP + s]
                acc[at] += products[n * CAP + s].astype(jnp.bfloat16).astype(jnp.float32)
        return carry

    lax.fori_loop(0, STEP // 2, one, 0)

    @pl.when(step == pl.num_programs(0) - 1)
    def _():
        out[...] = acc[...].astype(jnp.bfloat16)


def unsplat(ids, pieces, arrived, shape):
    peers = arrived.shape[0]
    return pl.pallas_call(
        unsplat_kernel,
        out_shape=jax.ShapeDtypeStruct(shape, jnp.bfloat16),
        grid=(peers // STEP,),
        in_specs=[
            SMEM(),
            pl.BlockSpec((4, STEP, CAP * PIECE, BLOCK), lambda i: (0, i, 0, 0)),
            pl.BlockSpec((STEP, CAP * SLOT, BLOCK), lambda i: (i, 0, 0)),
        ],
        out_specs=pl.BlockSpec(shape, lambda i: (0, 0, 0)),
        scratch_shapes=[pltpu.VMEM(shape, jnp.float32), pltpu.VMEM((2 * CAP,) + shape[1:], jnp.float32)],
        compiler_params=params(),
        name="unsplat",
    )(ids, pieces, arrived)


def paired(rows):
    rows = rows.reshape(4, 2, 10, LINE, 192)
    tails = jnp.concatenate([rows[:, 0, :, :, 128:], rows[:, 1, :, :, 128:]], axis=-1)
    return jnp.concatenate([rows[..., :128], tails[:, None]], axis=1)


def per_device(points, head_weight, teacher, splat_weight, block_owner, block_local, block_row):
    peers = lax.axis_size("view")
    feat = lax.axis_index("feat")
    local_width = points.shape[1]
    views, visible = splat_weight.shape[:2]
    requests = views * visible
    lines = views * GRID

    source, filled = slot_plan(block_owner.reshape(requests), peers, CAP)
    local = block_local.reshape(requests)
    line_of = (block_row + jnp.arange(views, dtype=jnp.int32)[:, None] * GRID).reshape(requests)

    mine = lax.dynamic_slice_in_dim(
        jnp.pad(splat_weight, ((0, 0), (0, 0), (0, 4 * PIECE - ROWS), (0, 0))), feat * PIECE, PIECE, axis=2
    ).reshape(requests, PIECE, BLOCK)
    packed, tags = pack_weights(source, filled, local, mine, peers)
    wanted = paired(
        jnp.pad(
            teacher.transpose(1, 2, 0).reshape(lines, GRID, local_width), ((0, 80 - lines), (0, LINE - GRID), (0, 0))
        )
    )

    arrived, pieces, tags_in, head, target = forward_exchange(packed, tags, points, head_weight, wanted)
    ids = tags_in[:, 0, :CAP].reshape(peers * CAP)
    image = render(source, line_of, arrived)
    landed, head_sum = backward_exchange(source, line_of, image, head, target, lines, peers)
    grad_points = unsplat(ids, pieces, landed, points.shape)
    columns = head_sum.reshape(6, local_width, BLOCK).astype(jnp.float32)
    tails = columns[4:].reshape(2, local_width, 2, 64).transpose(0, 2, 1, 3).reshape(4, local_width, 64)
    head_grad = jnp.concatenate([columns[:4], tails], axis=2).transpose(1, 0, 2).reshape(local_width, 4 * 192)
    return grad_points, head_grad / (views * peers * GRID)


def solution(mesh):
    placed = (
        P("view", "feat", None),
        P("feat", None),
        P("feat", "view", None),
        P("view", None, None, None),
        P("view", None, None),
        P("view", None),
        P("view", None),
    )
    return jax.shard_map(
        per_device,
        mesh=mesh,
        in_specs=placed,
        out_specs=(P("view", "feat", None), P("feat", None)),
        check_vma=False,
    )
```

```python
import functools

import jax
import jax.numpy as jnp
from jax import lax
from jax.experimental import pallas as pl
from jax.experimental.pallas import tpu as pltpu
from jax.sharding import PartitionSpec as P

GRID = 37
BAND = 2
BLOCK = 128
CAP = 3
ROWS = BAND * GRID
PIECE = 56
FORMS = 192
SLOT = 112
LINE = 40
STEP = 8
PLANE = 8
PAIRS = 40
STRIDE = 27
LAG = 12
MESH = pl.DeviceIdType.MESH
SMEM = functools.partial(pl.BlockSpec, memory_space=pltpu.SMEM)
NT = (((1,), (1,)), ((), ()))
TN = (((0,), (0,)), ((), ()))
VMEM_LIMIT = 60 * 1024 * 1024


def params(**kw):
    return pltpu.CompilerParams(vmem_limit_bytes=VMEM_LIMIT, **kw)


def slot_plan(owners, peer_count, capacity):
    total_requests = owners.shape[0]
    positions = jnp.arange(total_requests, dtype=jnp.int32)
    earlier = (owners[:, None] == owners[None, :]) & (positions[None, :] < positions[:, None])
    slot_rank = jnp.sum(earlier.astype(jnp.int32), axis=1)
    target = owners * capacity + slot_rank
    slot_ids = jnp.arange(peer_count * capacity, dtype=jnp.int32)
    matches = target[None, :] == slot_ids[:, None]
    return jnp.sum(jnp.where(matches, positions[None, :] + 1, 0), axis=1) - 1


def entry_of(source, t):
    return jnp.maximum(source[t], 0)


def line_at(rows, entry):
    view = entry // rows.shape[1]
    return rows[view, entry % rows.shape[1]] + view * GRID


def peer_at(me, i, peers):
    return (me + i * STRIDE) % peers


def greet(me, feat, peers):
    barrier = pltpu.get_barrier_semaphore()

    def hello(i, carry):
        pl.semaphore_signal(barrier, inc=1, device_id=(peer_at(me, i, peers), feat), device_id_type=MESH)
        return carry

    lax.fori_loop(1, peers, hello, 0)
    for k in range(1, 4):
        pl.semaphore_signal(barrier, inc=1, device_id=(me, (feat + k) % 4), device_id_type=MESH)


def remote(src, dst, send, recv, view, feat):
    return pltpu.make_async_remote_copy(
        src_ref=src, dst_ref=dst, send_sem=send, recv_sem=recv, device_id=(view, feat), device_id_type=MESH
    )


def wait_bytes(ref, sem):
    pltpu.make_async_copy(ref, ref, sem).wait()


def cut_lines(teacher, lines, wanted):
    patches = teacher.shape[1]
    whole = patches // 32
    for v in range(teacher.shape[0]):

        def widen(t, carry):
            at = pl.ds(pl.multiple_of(32 * t, 32), 32)
            lines[v, at, :] = teacher[v, at, :].astype(jnp.float32)
            return carry

        lax.fori_loop(0, whole, widen, 0)
        lines[v, 32 * whole : patches, :] = teacher[v, 32 * whole : patches, :].astype(jnp.float32)

    def line(n):
        v, r = n // GRID, n % GRID
        if v >= teacher.shape[0]:
            return jnp.zeros((LINE, 192), jnp.float32)
        return jnp.concatenate([lines[v, r * GRID : (r + 1) * GRID, :], jnp.zeros((LINE - GRID, 192), jnp.float32)], axis=0)

    for f in range(4):
        for m in range(10):
            first, second = line(20 * f + m), line(20 * f + 10 + m)
            wanted[f, 0, m] = first[:, 0:128].astype(jnp.bfloat16)
            wanted[f, 1, m] = second[:, 0:128].astype(jnp.bfloat16)
            wanted[f, 2, m] = jnp.concatenate([first[:, 128:192], second[:, 128:192]], axis=1).astype(jnp.bfloat16)


def forward_kernel(
    source, local, rows, weights, points_far, head_far, teacher_far, arrived, forms_out, tags_out, head_out, target, tables_in,
    packed, tags, tables, pieces, tags_in, tags_s, send, buf, joined, forms, form, head_in, head_turned, points, head, teacher, lines, wanted,
    w_send, w_recv, t_send, t_recv, l_sem, r_send, r_recv, c_send, c_recv, h_send, h_recv, y_send, y_recv, k_send, k_recv, own, load,
):
    me, feat = lax.axis_index("view"), lax.axis_index("feat")
    loads = [
        pltpu.make_async_copy(src, dst, load.at[n])
        for n, (src, dst) in enumerate(((points_far, points), (head_far, head), (teacher_far, teacher)))
    ]
    for one in loads:
        one.start()
    peers = packed.shape[0]
    lane = lax.broadcasted_iota(jnp.int32, (GRID, BLOCK), 1)
    row = lax.broadcasted_iota(jnp.int32, (1, BLOCK), 1)
    visible = local.shape[1]
    greet(me, feat, peers)

    def pack(p):
        tag = jnp.zeros((1, BLOCK), jnp.int32)
        for s in range(CAP):
            entry = entry_of(source, p * CAP + s)
            joined[s * ROWS : (s + 1) * ROWS, :] = jnp.where(
                source[p * CAP + s] >= 0, weights[entry].astype(jnp.float32), 0.0
            )
            tag = jnp.where(row == s, local[entry // visible, entry % visible], tag)
        packed[p] = joined[pl.ds(pl.multiple_of(feat * PIECE, 8), PIECE), :].astype(jnp.bfloat16)
        tags[p] = tag

    joined[...] = jnp.zeros_like(joined)
    form[...] = jnp.zeros_like(form)
    inside = lax.broadcasted_iota(jnp.int32, (80, BLOCK), 0) < ROWS
    pack(me)
    pack(peer_at(me, 1, peers))
    pl.semaphore_wait(pltpu.get_barrier_semaphore(), peers + 2)
    own_piece = pltpu.make_async_copy(packed.at[me], pieces.at[feat, me], own.at[0])
    own_piece.start()
    own_tag = pltpu.make_async_copy(tags.at[me], tags_in.at[me], own.at[1])
    own_tag.start()

    def weights_to(p, at):
        return remote(packed.at[p], pieces.at[feat, at], w_send, w_recv.at[at], p, feat)

    def tags_to(p, at):
        return remote(tags.at[p], tags_in.at[at], t_send, t_recv.at[at], p, feat)

    def relay(q, k):
        return remote(
            pieces.at[feat, q], pieces.at[feat, q], r_send.at[k - 1], r_recv.at[k - 1, q], me, (feat + k) % 4
        )

    def relayed(q, k):
        came = (feat + 4 - k) % 4
        return remote(pieces.at[came, q], pieces.at[came, q], r_send.at[k - 1], r_recv.at[k - 1, q], me, came)

    def tag_copy(q):
        return pltpu.make_async_copy(tags_in.at[q], tags_s.at[q], l_sem.at[q])

    def contrib_to(q):
        return remote(send.at[q], arrived.at[me], c_send, c_recv, q, feat)

    def give(p):
        tags_to(p, me).start()
        weights_to(p, me).start()

    def first(i, carry):
        pack(peer_at(me, i, peers))
        give(peer_at(me, i - 1, peers))
        return carry

    lax.fori_loop(2, peers, first, 0)
    planes = peers // PLANE
    level, place = me // PLANE, me % PLANE

    def fill(n, carry):
        def entry(t, table):
            line = line_at(rows, entry_of(source, n * PLANE * CAP + t))
            after = line + 1
            table = jnp.where(row == t, (line // 2) % 5 * 8 + line // 10, table)
            return jnp.where(row == t + PLANE * CAP, (after // 2) % 5 * 8 + after // 10, table)

        tables[n] = lax.fori_loop(0, PLANE * CAP, entry, jnp.zeros((1, BLOCK), jnp.int32))
        return carry

    lax.fori_loop(0, planes, fill, 0)
    give(peer_at(me, peers - 1, peers))

    def pass_on(q):
        for k in (1, 3, 2):
            relay(q, k).start()
        tag_copy(q).start()

    def stage_a(i, carry):
        q = peer_at(me, peers - i, peers)
        tags_to(q, q).wait_recv()
        weights_to(q, q).wait_recv()
        pass_on(q)
        return carry

    def product(q):
        for k in (1, 2, 3):
            relayed(q, k).wait_recv()
        tag_copy(q).wait()
        full = jnp.concatenate([pieces[f, q].astype(jnp.float32) for f in range(4)], axis=0)
        full = jnp.concatenate([full, jnp.zeros((8, BLOCK), jnp.float32)], axis=0)
        for s in range(CAP):
            rows_s = jnp.where(inside, full[s * ROWS : s * ROWS + 80], 0.0)
            form[s, GRID : GRID + ROWS, :] = rows_s[0:ROWS]
            form[s, SLOT : SLOT + GRID, :] = rows_s[0:GRID]
            form[s, SLOT + LINE : SLOT + LINE + GRID, :] = rows_s[GRID:ROWS]
            forms[q, pl.ds(s * FORMS, FORMS), :] = form[s].astype(jnp.bfloat16)
            block = points[tags_s[q, 0, s]]
            wide = jnp.concatenate([block, block[128:192]], axis=0)
            result = lax.dot_general(rows_s.astype(jnp.bfloat16), wide, NT, preferred_element_type=jnp.float32)
            rest = result[:, 128:256]
            buf[s, 0:80, :] = result[:, 0:128]
            buf[s, ROWS : ROWS + GRID, :] = jnp.where(lane < 64, rest[0:GRID], rest[GRID:ROWS])
            buf[s, SLOT - 1 : SLOT, :] = jnp.zeros((1, BLOCK), jnp.float32)
            send[q, pl.ds(s * SLOT, SLOT), :] = buf[s].astype(jnp.bfloat16)

    def stage_b(i, carry):
        product(peer_at(me, peers - i, peers))

        @pl.when(i > 1)
        def _():
            contrib_to(peer_at(me, peers - i + 1, peers)).start()

        return carry

    for one in loads:
        one.wait()
    own_piece.wait()
    own_tag.wait()
    pass_on(me)
    lax.fori_loop(1, LAG, stage_a, 0)

    def both(i, carry):
        stage_a(i, carry)
        return stage_b(i - LAG + 1, carry)

    lax.fori_loop(LAG, peers, both, 0)
    lax.fori_loop(peers - LAG + 1, peers, stage_b, 0)

    def head_to(k):
        return remote(head, head_in.at[feat], h_send.at[k - 1], h_recv.at[k - 1], me, (feat + k) % 4)

    def wanted_to(k):
        dst = (feat + k) % 4
        return remote(wanted.at[dst], target.at[feat], y_send.at[k - 1], y_recv.at[k - 1], me, dst)

    cut_lines(teacher, lines, wanted)

    def table_to(i):
        there = (level + i) % planes
        return remote(
            tables.at[there], tables_in.at[level], k_send.at[i - 1], k_recv.at[i - 1], there * PLANE + place, feat
        )

    for i in range(1, planes):
        table_to(i).start()
    own_table = pltpu.make_async_copy(tables.at[level], tables_in.at[level], own.at[5])
    own_table.start()
    for k in (1, 3, 2):
        head_to(k).start()
    for k in (1, 3, 2):
        wanted_to(k).start()
    own_head = pltpu.make_async_copy(head, head_in.at[feat], own.at[3])
    own_head.start()
    own_wanted = pltpu.make_async_copy(wanted.at[feat], target.at[feat], own.at[4])
    own_wanted.start()
    product(me)
    contrib_to(peer_at(me, 1, peers)).start()
    keep = pltpu.make_async_copy(forms, forms_out, own.at[0])
    keep.start()
    keep_tags = pltpu.make_async_copy(tags_in, tags_out, own.at[1])
    keep_tags.start()
    own_contrib = pltpu.make_async_copy(send.at[me], arrived.at[me], own.at[2])
    own_contrib.start()

    own_head.wait()
    for k in (1, 2, 3):
        head_to(k).wait_recv()

    def turn(f, carry):
        full = head_in[f].astype(jnp.float32)
        mains = [full[:, 192 * c : 192 * c + 128] for c in range(4)]
        tails = [full[:, 192 * c + 128 : 192 * c + 192] for c in range(4)]
        turned = jnp.concatenate(mains + tails, axis=1).astype(jnp.bfloat16)
        head_turned[f] = jnp.concatenate([turned, turned[128:192]], axis=0)
        return carry

    lax.fori_loop(0, 4, turn, 0)
    own_wanted.wait()
    own_table.wait()
    for i in range(1, planes):
        table_to(i).wait_send()
        table_to(i).wait_recv()
    for k in (1, 2, 3):
        head_to(k).wait_send()
        wanted_to(k).wait_send()
        wanted_to(k).wait_recv()
    others = pl.ds(0, peers - 1)
    keep_head = pltpu.make_async_copy(head_turned, head_out, own.at[3])
    keep_head.start()
    wait_bytes(packed.at[others], w_send)
    wait_bytes(tags.at[others], t_send)
    for k in range(3):
        wait_bytes(packed, r_send.at[k])
    wait_bytes(send.at[others], c_send)
    wait_bytes(send.at[others], c_recv)
    keep.wait()
    keep_tags.wait()
    own_contrib.wait()
    keep_head.wait()


def forward_exchange(source, local, rows, weights, points, head, teacher, peers):
    whole = pl.BlockSpec(memory_space=pltpu.VMEM)
    dma = pltpu.SemaphoreType.DMA
    slots, wanted = (peers, CAP * SLOT, BLOCK), (4, 3, 10, LINE, BLOCK)
    forms, doubled = (peers, CAP * FORMS, BLOCK), (4, 256, head.shape[1])
    packed, tags, tables = (peers, PIECE, BLOCK), (peers, 1, BLOCK), (peers // PLANE, 1, BLOCK)
    return pl.pallas_call(
        forward_kernel,
        out_shape=(
            jax.ShapeDtypeStruct(slots, jnp.bfloat16),
            jax.ShapeDtypeStruct(forms, jnp.bfloat16),
            jax.ShapeDtypeStruct(tags, jnp.int32),
            jax.ShapeDtypeStruct(doubled, jnp.bfloat16),
            jax.ShapeDtypeStruct(wanted, jnp.bfloat16),
            jax.ShapeDtypeStruct(tables, jnp.int32),
        ),
        in_specs=[SMEM()] * 3 + [whole] + [pl.BlockSpec(memory_space=pl.ANY)] * 3,
        out_specs=(pl.BlockSpec(memory_space=pl.ANY),) * 6,
        scratch_shapes=[
            pltpu.VMEM(packed, jnp.bfloat16),
            pltpu.VMEM(tags, jnp.int32),
            pltpu.VMEM(tables, jnp.int32),
            pltpu.VMEM((4,) + packed, jnp.bfloat16),
            pltpu.VMEM(tags, jnp.int32),
            pltpu.SMEM(tags, jnp.int32),
            pltpu.VMEM(slots, jnp.bfloat16),
            pltpu.VMEM((CAP, SLOT, BLOCK), jnp.float32),
            pltpu.VMEM((4 * PIECE, BLOCK), jnp.float32),
            pltpu.VMEM(forms, jnp.bfloat16),
            pltpu.VMEM((CAP, FORMS, BLOCK), jnp.float32),
            pltpu.VMEM((4,) + head.shape, jnp.bfloat16),
            pltpu.VMEM(doubled, jnp.bfloat16),
            pltpu.VMEM(points.shape, jnp.bfloat16),
            pltpu.VMEM(head.shape, jnp.bfloat16),
            pltpu.VMEM(teacher.shape, jnp.bfloat16),
            pltpu.VMEM(teacher.shape, jnp.float32),
            pltpu.VMEM(wanted, jnp.bfloat16),
            dma, dma((peers,)), dma, dma((peers,)), dma((peers,)),
            dma((3,)), dma((3, peers)), dma, dma,
            dma((3,)), dma((3,)), dma((3,)), dma((3,)), dma((7,)), dma((7,)), dma((6,)), dma((3,)),
        ],
        compiler_params=params(collective_id=0, has_side_effects=True),
        name="forward_exchange",
    )(source, local, rows, weights, points, head, teacher)


def render_kernel(source, rows, arrived, out, acc):
    step = pl.program_id(0)
    lane = lax.broadcasted_iota(jnp.int32, (GRID, BLOCK), 1)

    @pl.when(step == 0)
    def _():
        acc[...] = jnp.zeros_like(acc)

    def one(i, carry):
        for s in range(CAP):
            at = line_at(rows, entry_of(source, (step * STEP + i) * CAP + s)) + 1
            acc[at] += arrived[i, pl.ds(s * SLOT, SLOT), :].astype(jnp.float32)
        return carry

    lax.fori_loop(0, STEP, one, 0, unroll=2)

    @pl.when(step == pl.num_programs(0) - 1)
    def _():
        out[...] = jnp.zeros_like(out)
        pairs = pl.ds(ROWS, GRID)

        def finish(k, carry):
            f, m = k // 10, k % 10
            for half in range(2):
                at = f * 20 + half * 10 + m
                out[f, half, m, 0:GRID, :] = (acc[at + 1, 0:GRID, :] + acc[at, GRID:ROWS, :]).astype(jnp.bfloat16)
            low, high = f * 20 + m, f * 20 + 10 + m
            turned = pltpu.roll(jnp.where(lane < 64, acc[high + 1, pairs, :], acc[low, pairs, :]), 64, 1)
            straight = jnp.where(lane < 64, acc[low + 1, pairs, :], acc[high, pairs, :])
            out[f, 2, m, 0:GRID, :] = (turned + straight).astype(jnp.bfloat16)
            return carry

        lax.fori_loop(0, 40, finish, 0, unroll=2)


def render(source, rows, arrived):
    peers = arrived.shape[0]
    shape = (4, 3, 10, LINE, BLOCK)
    return pl.pallas_call(
        render_kernel,
        out_shape=jax.ShapeDtypeStruct(shape, jnp.bfloat16),
        grid=(peers // STEP,),
        in_specs=[SMEM(), SMEM(), pl.BlockSpec((STEP, CAP * SLOT, BLOCK), lambda i: (i, 0, 0))],
        out_specs=pl.BlockSpec(shape, lambda i: (0, 0, 0, 0, 0)),
        scratch_shapes=[pltpu.VMEM((81, SLOT, BLOCK), jnp.float32)],
        compiler_params=params(),
        name="render",
    )(source, rows, arrived)


def widened(image, f, start, lines):
    count = lines * LINE
    lane = lax.broadcasted_iota(jnp.int32, (count, BLOCK), 1)
    parts = [image[f, j, pl.ds(start, lines)].reshape(count, BLOCK) for j in range(3)]
    zero = jnp.zeros_like(parts[2])
    upper = jnp.concatenate([parts[0], jnp.where(lane < 64, parts[2], zero)], axis=1)
    lower = jnp.concatenate([parts[1], jnp.where(lane < 64, zero, parts[2])], axis=1)
    return jnp.concatenate([upper, lower], axis=0)


def target_rows(target, start, lines):
    count = lines * LINE
    lane = lax.broadcasted_iota(jnp.int32, (count, BLOCK), 1)
    part = [
        [target[f, j, pl.ds(start, lines)].reshape(count, BLOCK).astype(jnp.float32) for j in range(3)] for f in range(4)
    ]
    halves = []
    for half in range(2):
        row = [part[f][half] for f in range(4)]
        for f in (0, 2):
            first, second = part[f][2], part[f + 1][2]
            if half == 0:
                second = pltpu.roll(second, 64, 1)
            else:
                first = pltpu.roll(first, 64, 1)
            row.append(jnp.where(lane < 64, first, second))
        halves.append(jnp.concatenate(row, axis=1))
    return jnp.concatenate(halves, axis=0)


def compare_chunk(g, rendered, head, target, grad_image, grad_proj):
    count, width = 2 * LINE, head.shape[-1]
    lane = lax.broadcasted_iota(jnp.int32, (count, BLOCK), 1)
    projected = jnp.zeros((2 * count, width), jnp.float32)
    for f in range(4):
        projected += jnp.dot(widened(rendered, f, 2 * g, 2), head[f], preferred_element_type=jnp.float32)
    scale = jnp.sqrt(jnp.sum(projected * projected, axis=1, keepdims=True) / width + 1e-06)
    inverse = 1.0 / scale
    normed = projected * inverse
    residual = normed - target_rows(target, 2 * g, 2)
    row_dot = jnp.sum(residual * normed, axis=1, keepdims=True) / width
    grad = ((residual - normed * row_dot) * inverse).astype(jnp.bfloat16)
    grad_proj[:, pl.ds(2 * g, 2)] = grad.reshape(2, 2, LINE, width)
    for f in range(4):
        image = lax.dot_general(grad, head[f], NT, preferred_element_type=jnp.float32)
        for half in range(2):
            main = image[half * count : (half + 1) * count, 0:128]
            grad_image[f, half, pl.ds(2 * g, 2)] = main.astype(jnp.bfloat16).reshape(2, LINE, BLOCK)
        pairs = jnp.where(lane < 64, image[0:count, 128:256], image[count : 2 * count, 128:256])
        grad_image[f, 2, pl.ds(2 * g, 2)] = pairs.astype(jnp.bfloat16).reshape(2, LINE, BLOCK)


def head_product(f, rendered, grad_proj, out):
    rows = widened(rendered, f, 0, 10)
    for j in range(3):
        grad = grad_proj[:, :, :, j * 256 : (j + 1) * 256].reshape(rows.shape[0], 256)
        part = lax.dot_general(rows, grad, TN, preferred_element_type=jnp.float32)
        for h in range(2):
            cols = part[:, h * 128 : (h + 1) * 128]
            full = jnp.concatenate([cols[0:128], cols[128:192] + cols[192:256]], axis=0)
            out[f, :, 2 * j + h] = full.reshape(PLANE, 24, BLOCK)


def build_pairs(g, image, pairs, buf):
    lane = lax.broadcasted_iota(jnp.int32, (GRID, BLOCK), 1)
    for seg in range(8):
        f, half, slot = seg // 2, seg % 2, seg % 2
        mains = [image[f, half, 2 * g + n].astype(jnp.float32)[0:GRID] for n in range(2)]
        tails = [image[f, 2, 2 * g + n].astype(jnp.float32)[0:GRID] for n in range(2)]
        tails[1 - half] = pltpu.roll(tails[1 - half], 64, 1)
        buf[slot, 0:GRID, :] = jnp.where(lane < 64, tails[0], tails[1])
        buf[slot, GRID:ROWS, :] = mains[0]
        buf[slot, ROWS : ROWS + GRID, :] = mains[1]
        pairs[8 * g + seg] = buf[slot].astype(jnp.bfloat16)


def backward_kernel(
    head_count, table, image, head_far, target_far, landed, head_out,
    rendered, grad_image, grad_in, grad_proj, head_part,
    own_pairs, up_1, up_2, up_3, down_1, down_2, down_3, far_pairs, buf,
    send, head_in, share, plane_in, level_sum, level_in, total, total_in, all_in, head_rows, head, target,
    p_send, p_recv, q_send, q_recv, z_send, z_recv,
    g_send, g_recv, x_send, x_recv, a_send, a_recv, c_send, c_recv, d_send, d_recv, e_send, e_recv, own, kept, load,
):
    me, feat = lax.axis_index("view"), lax.axis_index("feat")
    planes = level_in.shape[0] + 1
    held = ((own_pairs, up_1, up_2, up_3, far_pairs), (own_pairs, down_1, down_2, down_3, far_pairs))
    level, place = me // PLANE, me % PLANE
    lane = lax.broadcasted_iota(jnp.int32, (GRID, BLOCK), 1)
    own_image = pltpu.make_async_copy(image.at[feat], rendered.at[feat], own.at[0])
    own_image.start()
    loads = [
        pltpu.make_async_copy(src, dst, load.at[n])
        for n, (src, dst) in enumerate(((head_far, head), (target_far, target)))
    ]
    for one in loads:
        one.start()

    def at_level(i):
        return ((level + i) % planes) * PLANE + place

    def in_plane(i):
        return level * PLANE + (place + i) % PLANE

    barrier = pltpu.get_barrier_semaphore()
    for k in range(1, 4):
        pl.semaphore_signal(barrier, inc=1, device_id=(me, (feat + k) % 4), device_id_type=MESH)
    for i in range(1, planes):
        pl.semaphore_signal(barrier, inc=1, device_id=(at_level(i), feat), device_id_type=MESH)
    for i in range(1, PLANE):
        pl.semaphore_signal(barrier, inc=1, device_id=(in_plane(i), feat), device_id_type=MESH)
    pl.semaphore_wait(barrier, 3 + planes - 1 + PLANE - 1)

    def image_to(k, g):
        dst, chunk = (feat + k) % 4, pl.ds(2 * g, 2)
        return remote(
            image.at[dst, :, chunk], rendered.at[feat, :, chunk], p_send.at[k - 1, g], p_recv.at[k - 1, g], me, dst
        )

    def grads_back(k, g):
        dst, chunk = (feat + k) % 4, pl.ds(2 * g, 2)
        return remote(
            grad_image.at[dst, :, chunk], grad_in.at[feat, :, chunk], q_send.at[k - 1, g], q_recv.at[k - 1, g], me, dst
        )

    def own_back(g):
        chunk = pl.ds(2 * g, 2)
        return pltpu.make_async_copy(grad_image.at[feat, :, chunk], grad_in.at[feat, :, chunk], kept.at[g])

    def each_size(g, act):
        @pl.when(g < 2)
        def _():
            act(8)

        @pl.when(g >= 2)
        def _():
            act(7)

    def ring(way, hop, g, count):
        chunk = pl.ds(8 * g, count)
        src, dst = held[way][hop].at[chunk], held[way][hop + 1].at[chunk]
        return remote(src, dst, z_send.at[way, hop, g], z_recv.at[way, hop, g], at_level(planes + 1 - 2 * way), feat)

    def ring_send(way, hop, g):
        each_size(g, lambda count: ring(way, hop, g, count).start())

    def ring_wait(way, hop, g):
        each_size(g, lambda count: ring(way, hop, g, count).wait_recv())

    def ring_sent(way, hop, g):
        each_size(g, lambda count: ring(way, hop, g, count).wait_send())

    def hand_out(g, carry):
        for k in (1, 3, 2):
            image_to(k, g).start()
        return carry

    lax.fori_loop(0, 5, hand_out, 0)
    buf[...] = jnp.zeros_like(buf)
    own_image.wait()
    for one in loads:
        one.wait()

    def returned(g):
        own_back(g).wait()
        for k in (1, 2, 3):
            grads_back(k, g).wait_recv()
        build_pairs(g, grad_in, own_pairs, buf)
        ring_send(0, 0, g)
        ring_send(1, 0, g)

    def chunk_step(g, carry):
        for k in (1, 2, 3):
            image_to(k, g).wait_recv()
        compare_chunk(g, rendered, head, target, grad_image, grad_proj)
        own_back(g).start()
        for k in (1, 3, 2):
            grads_back(k, g).start()

        @pl.when(g > 0)
        def _():
            returned(g - 1)

        return carry

    lax.fori_loop(0, 5, chunk_step, 0)
    returned(4)

    def grads_to(origin, i):
        return remote(
            send.at[origin * PLANE + (place + i) % PLANE], landed.at[origin * PLANE + place], g_send, g_recv, in_plane(i), feat
        )

    def pack(origin, pairs, i):
        to = (place + i) % PLANE
        for s in range(CAP):
            first, second = table[origin, 0, to * CAP + s], table[origin, 0, PLANE * CAP + to * CAP + s]
            own_pair = pairs[first].astype(jnp.float32)
            next_pair = pairs[second].astype(jnp.float32)
            buf[s, 0:GRID, :] = pltpu.roll(jnp.where(lane < 64, next_pair[0:GRID], own_pair[0:GRID]), 64, 1)
            buf[s, GRID:ROWS, :] = own_pair[ROWS : ROWS + GRID]
            buf[s, ROWS : ROWS + GRID, :] = next_pair[GRID:ROWS]
            slot = jnp.where(first == second, own_pair, buf[s])
            send[origin * PLANE + to, pl.ds(s * SLOT, SLOT), :] = slot.astype(jnp.bfloat16)

    def deal(origins, start, stop):
        def one(i, carry):
            for origin, pairs in origins:
                pack(origin, pairs, i)

            @pl.when(i > 0)
            def _():
                for origin, _ in origins:
                    grads_to(origin, i).start()

            return carry

        lax.fori_loop(start, stop, one, 0)

    def both_at(d):
        return (((level + planes - d) % planes, held[0][d]), ((level + d) % planes, held[1][d]))

    def head_step(f, carry):
        head_product(f, rendered, grad_proj, head_part)
        return carry

    def across(k):
        return remote(head_part.at[(feat + k) % 4], head_in.at[k - 1], x_send.at[k - 1], x_recv.at[k - 1], me, (feat + k) % 4)

    def share_to(i):
        return remote(share.at[(place + i) % PLANE], plane_in.at[i - 1], a_send.at[i - 1], a_recv.at[i - 1], in_plane(i), feat)

    owners = total_in.shape[0]

    def level_to(i):
        there = (level + i) % planes
        return remote(level_sum.at[there], level_in.at[i - 1], c_send.at[i - 1], c_recv.at[i - 1], at_level(i), feat)

    def total_to(i, origin):
        return remote(total, total_in.at[origin], d_send.at[i - 1], d_recv.at[i - 1], at_level(i), feat)

    def all_to(i, origin):
        return remote(total_in, all_in.at[origin], e_send.at[i - 1], e_recv.at[i - 1], in_plane(i), feat)

    def came_down(g, d, last):
        up, down = g < 2, g >= 2
        ring_wait(0, d - 1, g)
        if last:
            pl.when(up)(lambda: ring_send(0, d, g))
        else:
            ring_send(0, d, g)
        ring_wait(1, d - 1, g)
        if last:
            pl.when(down)(lambda: ring_send(1, d, g))
        else:
            ring_send(1, d, g)

    def first_step(g, carry):
        came_down(g, 1, False)
        return carry

    deal(((level, own_pairs),), 0, PLANE)
    lax.fori_loop(0, 4, head_step, 0)
    for k in (1, 3, 2):
        across(k).start()
    lax.fori_loop(0, 5, first_step, 0)
    deal(both_at(1), 0, PLANE)

    for k in (1, 2, 3):
        across(k).wait_recv()

    def add(t, carry):
        share[t] = head_part[feat, t] + head_in[0, t] + head_in[1, t] + head_in[2, t]
        return carry

    lax.fori_loop(0, PLANE, add, 0)

    def second_step(g, carry):
        came_down(g, 2, False)
        return carry

    lax.fori_loop(0, 1, second_step, 0)
    for i in range(1, PLANE):
        share_to(i).start()
    lax.fori_loop(1, 5, second_step, 0)
    deal(both_at(2), 0, PLANE)

    for i in range(1, PLANE):
        share_to(i).wait_recv()
    value = share[place]
    for i in range(PLANE - 1):
        value += plane_in[i]
    level_sum[...] = value

    def third_step(g, carry):
        came_down(g, 3, True)
        return carry

    lax.fori_loop(0, 1, third_step, 0)
    for i in range(1, planes):
        pl.when((level + i) % planes < owners)(lambda i=i: level_to(i).start())
    lax.fori_loop(1, 5, third_step, 0)
    deal(both_at(3), 0, PLANE)

    @pl.when(level < owners)
    def _():
        for i in range(1, planes):
            came = remote(level_sum.at[level], level_in.at[i - 1], c_send.at[i - 1], c_recv.at[i - 1], at_level(i), feat)
            came.wait_recv()
        value = level_sum[level]
        for i in range(planes - 1):
            value += level_in[i]
        total[...] = value

    def fourth_step(g, carry):
        up, down = g < 2, g >= 2
        pl.when(up)(lambda: ring_wait(0, 3, g))
        pl.when(down)(lambda: ring_wait(1, 3, g))
        return carry

    lax.fori_loop(0, 1, fourth_step, 0)

    @pl.when(level < owners)
    def _():
        for i in range(1, planes):
            total_to(i, level).start()
        mine = pltpu.make_async_copy(total, total_in.at[level], own.at[1])
        mine.start()
        mine.wait()

    lax.fori_loop(1, 5, fourth_step, 0)
    deal((((level + 4) % planes, far_pairs),), 0, PLANE)

    def own_slots(origin):
        at = origin * PLANE + place
        return pltpu.make_async_copy(send.at[at], landed.at[at], kept.at[origin])

    for origin in range(planes):
        own_slots(origin).start()
    for i in range(1, planes):
        origin = (level + planes - i) % planes
        pl.when(origin < owners)(lambda i=i, origin=origin: total_to(i, origin).wait_recv())
    for i in range(1, PLANE):
        all_to(i, place).start()
    mine = pltpu.make_async_copy(total_in, all_in.at[place], own.at[1])
    mine.start()
    mine.wait()
    for i in range(1, PLANE):
        all_to(i, (place + PLANE - i) % PLANE).wait_recv()

    def arrange(u, carry):
        parts = []
        for f in range(4):
            tail = all_in[u, 4 + f // 2]
            parts += [all_in[u, f], tail[:, 64 * (f % 2) : 64 * (f % 2) + 64]]
        head_rows[pl.ds(pl.multiple_of(24 * u, 8), 24), :] = jnp.concatenate(parts, axis=1) / head_count
        return carry

    lax.fori_loop(0, PLANE, arrange, 0)

    def drain(g, carry):
        for k in (1, 2, 3):
            image_to(k, g).wait_send()
            grads_back(k, g).wait_send()
        for way in range(2):
            for hop in range(3):
                ring_sent(way, hop, g)
        pl.when(g < 2)(lambda: ring_sent(0, 3, g))
        pl.when(g >= 2)(lambda: ring_sent(1, 3, g))
        return carry

    lax.fori_loop(0, 5, drain, 0)
    for k in (1, 2, 3):
        across(k).wait_send()
    for i in range(1, PLANE):
        share_to(i).wait_send()
        all_to(i, place).wait_send()
    for i in range(1, planes):
        pl.when((level + i) % planes < owners)(lambda i=i: level_to(i).wait_send())
        pl.when(level < owners)(lambda i=i: total_to(i, level).wait_send())
    others = pl.ds(0, planes * (PLANE - 1))
    result = pltpu.make_async_copy(head_rows, head_out, own.at[1])
    result.start()
    wait_bytes(send.at[others], g_send)
    wait_bytes(send.at[others], g_recv)
    for origin in range(planes):
        own_slots(origin).wait()
    result.wait()


def backward_exchange(table, image, head, target, peers, head_count):
    whole = pl.BlockSpec(memory_space=pltpu.VMEM)
    dma = pltpu.SemaphoreType.DMA
    planes, owners, tile = peers // PLANE, 6, (24, BLOCK)
    shape = (peers, CAP * SLOT, BLOCK)
    share = (PLANE, owners) + tile
    return pl.pallas_call(
        functools.partial(backward_kernel, float(head_count)),
        out_shape=(
            jax.ShapeDtypeStruct(shape, jnp.bfloat16),
            jax.ShapeDtypeStruct((192, head.shape[-1]), jnp.float32),
        ),
        in_specs=[SMEM(), whole, pl.BlockSpec(memory_space=pl.ANY), pl.BlockSpec(memory_space=pl.ANY)],
        out_specs=(pl.BlockSpec(memory_space=pl.ANY),) * 2,
        scratch_shapes=[
            pltpu.VMEM(image.shape, jnp.bfloat16),
            pltpu.VMEM(image.shape, jnp.bfloat16),
            pltpu.VMEM(image.shape, jnp.bfloat16),
            pltpu.VMEM((2, 10, LINE, head.shape[-1]), jnp.bfloat16),
            pltpu.VMEM((4,) + share, jnp.float32),
            *[pltpu.VMEM((PAIRS, SLOT, BLOCK), jnp.bfloat16)] * planes,
            pltpu.VMEM((CAP, SLOT, BLOCK), jnp.float32),
            pltpu.VMEM(shape, jnp.bfloat16),
            pltpu.VMEM((3,) + share, jnp.float32),
            pltpu.VMEM(share, jnp.float32),
            pltpu.VMEM((PLANE - 1, owners) + tile, jnp.float32),
            pltpu.VMEM((owners,) + tile, jnp.float32),
            pltpu.VMEM((planes - 1,) + tile, jnp.float32),
            pltpu.VMEM(tile, jnp.float32),
            pltpu.VMEM((owners,) + tile, jnp.float32),
            pltpu.VMEM(share, jnp.float32),
            pltpu.VMEM((192, head.shape[-1]), jnp.float32),
            pltpu.VMEM(head.shape, jnp.bfloat16),
            pltpu.VMEM(target.shape, jnp.bfloat16),
            dma((3, 5)), dma((3, 5)), dma((3, 5)), dma((3, 5)), dma((2, 4, 5)), dma((2, 4, 5)),
            dma, dma, dma((3,)), dma((3,)), dma((7,)), dma((7,)), dma((7,)), dma((7,)),
            dma((7,)), dma((7,)), dma((7,)), dma((7,)), dma((2,)), dma((8,)), dma((2,)),
        ],
        compiler_params=params(collective_id=1, has_side_effects=True),
        name="backward_exchange",
    )(table, image, head, target)


def unsplat_kernel(tags, forms, arrived, out, acc, products):
    step = pl.program_id(0)

    @pl.when(step == 0)
    def _():
        acc[...] = jnp.zeros_like(acc)

    def product(i, s, at):
        slot, base = arrived[i, pl.ds(s * SLOT, SLOT), :], s * FORMS
        main = lax.dot_general(slot, forms[i, pl.ds(base, SLOT), :], TN, preferred_element_type=jnp.float32)
        both = [forms[i, pl.ds(base + SLOT + n * LINE, LINE), :] for n in range(2)]
        rest = lax.dot_general(slot[0:LINE], jnp.concatenate(both, axis=1), TN, preferred_element_type=jnp.float32)
        products[at, 0:128, :] = main.astype(jnp.bfloat16)
        products[at, 128:192, :] = (rest[0:64, 0:128] + rest[64:128, 128:256]).astype(jnp.bfloat16)

    def one(i, carry):
        for n in range(STEP):
            for s in range(CAP):
                product(n, s, n * CAP + s)
        for n in range(STEP):
            for s in range(CAP):
                acc[tags[step * STEP + n, 0, s]] += products[n * CAP + s].astype(jnp.float32)
        return carry

    lax.fori_loop(0, 1, one, 0)

    @pl.when(step == pl.num_programs(0) - 1)
    def _():
        out[...] = acc[...].astype(jnp.bfloat16)


def unsplat(tags, forms, arrived, shape):
    peers = arrived.shape[0]
    return pl.pallas_call(
        unsplat_kernel,
        out_shape=jax.ShapeDtypeStruct(shape, jnp.bfloat16),
        grid=(peers // STEP,),
        in_specs=[
            SMEM(),
            pl.BlockSpec((STEP, CAP * FORMS, BLOCK), lambda i: (i, 0, 0)),
            pl.BlockSpec((STEP, CAP * SLOT, BLOCK), lambda i: (i, 0, 0)),
        ],
        out_specs=pl.BlockSpec(shape, lambda i: (0, 0, 0)),
        scratch_shapes=[pltpu.VMEM(shape, jnp.float32), pltpu.VMEM((STEP * CAP,) + shape[1:], jnp.bfloat16)],
        compiler_params=params(),
        name="unsplat",
    )(tags, forms, arrived)


def per_device(points, head_weight, teacher, splat_weight, block_owner, block_local, block_row):
    peers = lax.axis_size("view")
    views, visible = splat_weight.shape[:2]
    requests = views * visible

    source = slot_plan(block_owner.reshape(requests), peers, CAP)
    weights = splat_weight.reshape(requests, ROWS, BLOCK)
    arrived, forms, tags, head, target, table = forward_exchange(
        source, block_local, block_row, weights, points, head_weight, teacher.transpose(1, 2, 0), peers
    )
    image = render(source, block_row, arrived)
    landed, head_grad = backward_exchange(table, image, head, target, peers, views * peers * GRID)
    return unsplat(tags, forms, landed, points.shape), head_grad


def solution(mesh):
    placed = (
        P("view", "feat", None),
        P("feat", None),
        P("feat", "view", None),
        P("view", None, None, None),
        P("view", None, None),
        P("view", None),
        P("view", None),
    )
    return jax.shard_map(
        per_device,
        mesh=mesh,
        in_specs=placed,
        out_specs=(P("view", "feat", None), P("feat", None)),
        check_vma=False,
    )
```
